256 devices in a mesh: prow: 8 (over z), pcol: 32 (over x, y, core).
Axes of the slice: x: 4, y: 4, z: 8, core: 2. Of those that a mesh axis runs over, the one named last changes fastest.
Arguments:
- matrix: bfloat16 [8, 2048, 2, 8192], P(None, 'prow', None, 'pcol'), may hold values from -6 to 6
- pivots: int32 [4, 256], replicated, may hold values from 0 to 16383, as said below
- lower_inverse: bfloat16 [4, 256, 256], replicated, as said below
- upper_inverse: bfloat16 [4, 256, 256], replicated, as said below
Outputs:
- factored: bfloat16 [8, 2048, 2, 8192], P(None, 'prow', None, 'pcol')
The draws below stay inside these ranges and needn't reach their ends.
Inputs may be any that keep to these rules, and one draw needn't show every extreme that they name: For step s and each i, pivots[s, i] is either s * 256 + i or a row index of s * 256 + 256 or more; the pivots of one step that differ from s * 256 + i are distinct. lower_inverse[s] is unit lower triangular. upper_inverse[s] is upper triangular.
All inputs are finite; a program needn't handle non-finite values.
Results may differ from the reference program's by a relative error of at most 0.0071.
Values may be sent and summed in bfloat16 or wider, within the bound.
A program may use at most 64 MiB of HBM per device.

```python
import jax
import jax.numpy as jnp
from jax import lax

NB = 256
CB = 2
STEPS = 4
RB = 8
M = 16384
N_PROW = 8
N_PCOL = 32


def draw_pivots(key, part):
    stacked_rows = []
    for step_num in range(STEPS):
        step_key = jax.random.fold_in(key, step_num + 11)
        key_one, key_two = jax.random.split(step_key)
        lowest = (step_num + 1) * NB
        shuffled = jax.random.permutation(key_one, M - lowest).astype(jnp.int32)
        top_value = M - lowest - 1
        top_place = jnp.argmax(shuffled == top_value).astype(jnp.int32)
        second = shuffled[1]
        shuffled = shuffled.at[top_place].set(second).at[1].set(top_value)
        picked = lowest + shuffled[:NB]
        staying = jax.random.randint(key_two, (NB,), 0, 4) == 0
        staying = staying.at[1].set(False)
        if step_num == 0:
            staying = staying.at[0].set(True)
        own_rows = step_num * NB + jnp.arange(NB, dtype=jnp.int32)
        stacked_rows.append(jnp.where(staying, own_rows, picked.astype(jnp.int32)))
    return jnp.stack(stacked_rows).astype(jnp.int32)


def draw_upper_inverse(key, part):
    key_one, key_two = jax.random.split(jax.random.fold_in(key, 23))
    off_part = jax.random.normal(key_one, (STEPS, NB, NB), jnp.float32) / NB
    diag_part = jax.random.uniform(key_two, (STEPS, NB), jnp.float32, 0.5, 1.0)
    row_pos = lax.broadcasted_iota(jnp.int32, (NB, NB), 0)
    col_pos = lax.broadcasted_iota(jnp.int32, (NB, NB), 1)
    above = jnp.where(col_pos > row_pos, off_part, 0.0)
    on_diag = jnp.where(row_pos == col_pos, diag_part[:, :, None], 0.0) / NB ** 0.5
    return ((above + on_diag) * 0.25).astype(jnp.bfloat16)


def draw_lower_inverse(key, part):
    key_one = jax.random.fold_in(key, 37)
    off_part = jax.random.normal(key_one, (STEPS, NB, NB), jnp.float32) * 0.3 / NB ** 0.5
    row_pos = lax.broadcasted_iota(jnp.int32, (NB, NB), 0)
    col_pos = lax.broadcasted_iota(jnp.int32, (NB, NB), 1)
    below = jnp.where(row_pos > col_pos, off_part, 0.0)
    on_diag = jnp.where(row_pos == col_pos, 1.0, 0.0)
    return (below + on_diag).astype(jnp.bfloat16)


def block_levels(own_key, dims, pieces, least, high):
    def one(axis_at, blocks):
        draws = jax.random.uniform(jax.random.fold_in(jax.random.fold_in(own_key, 6), axis_at), (blocks,), jnp.float32, least / len(pieces), high / len(pieces))
        return jnp.repeat(jnp.exp(draws), dims[axis_at] // blocks).reshape((-1,) + (1,) * (len(dims) - axis_at - 1))

    factor_of = one(*pieces[0])
    for cut in pieces[1:]:
        factor_of = factor_of * one(*cut)
    return factor_of


def centred(stream_key, shape, width, limit, shards=(), kind=jnp.bfloat16):
    result = jax.random.normal(stream_key, shape, jnp.float32) * width
    if len(shards) > 0:
        result = block_levels(stream_key, shape, shards, -0.22, 0.18) * result
    return jnp.clip(result, min=-limit, max=limit).astype(kind)


def setup_inputs(seed: int = 0) -> dict:
    keys = jax.random.split(jax.random.key(seed), 5)
    return {
        "matrix": centred(keys[0], (RB, N_PROW * NB, CB, N_PCOL * NB), 1.0, 6.0, ((1, 8), (3, 32))),
        "pivots": draw_pivots(jax.random.fold_in(keys[4], 71), 0),
        "lower_inverse": draw_lower_inverse(jax.random.fold_in(keys[4], 71), 0),
        "upper_inverse": draw_upper_inverse(jax.random.fold_in(keys[4], 71), 0),
    }


def reference(matrix, pivots, lower_inverse, upper_inverse):
    whole = matrix.reshape(M, M)
    for step_num in range(STEPS):
        begin_at = step_num * NB
        trail_at = begin_at + NB
        targets = begin_at + jnp.arange(NB, dtype=jnp.int32)
        chosen = pivots[step_num].astype(jnp.int32)
        order_map = jnp.arange(M, dtype=jnp.int32).at[chosen].set(targets).at[targets].set(chosen)
        whole = whole[order_map]
        left_block = jnp.dot(whole[trail_at:, begin_at:trail_at], upper_inverse[step_num], preferred_element_type=jnp.float32).astype(jnp.bfloat16)
        upper_block = jnp.dot(lower_inverse[step_num], whole[begin_at:trail_at, trail_at:], preferred_element_type=jnp.float32).astype(jnp.bfloat16)
        corner = (whole[trail_at:, trail_at:].astype(jnp.float32) - jnp.dot(left_block, upper_block, preferred_element_type=jnp.float32)).astype(jnp.bfloat16)
        whole = whole.at[trail_at:, begin_at:trail_at].set(left_block)
        whole = whole.at[begin_at:trail_at, trail_at:].set(upper_block)
        whole = whole.at[trail_at:, trail_at:].set(corner)
    return whole.reshape(matrix.shape)
```

```python
import jax
import jax.numpy as jnp
from jax import lax
from jax.experimental import pallas as pl
from jax.experimental.pallas import tpu as pltpu
from jax.sharding import PartitionSpec as P

BF = jnp.bfloat16
F32 = jnp.float32
NB = 256
NZ = 8
TOP = 1024
COLS = 512


def dot(a, b):
    return jnp.dot(a, b, preferred_element_type=F32)


def kernel(a_ref, piv_ref, linv_ref, uinv_ref, out_ref,
           srcb, destr, contrib, rs_long, rs_short, top_own, old_own, pan, top_pan,
           left, tx, ux,
           sem_rs, rem_rs, sem_tz, rem_tz, sem_dz, rem_dz,
           sem_sc, rem_sc, sem_mir, rem_mir, loc_sem, sem_ds, rem_ds,
           sem_ts, rem_ts, sem_tsl, rem_tsl,
           sem_ring, rem_ring, sem_par, rem_par):
    r = lax.axis_index("prow")
    q = lax.axis_index("pcol")
    x = q // 8
    y = (q // 2) % 4
    core = q % 2
    g = core * 4 + x

    def panel_of(yy):
        return (yy % 3 + 1) * ((yy + 3) // 4)

    p = panel_of(y)
    home_y = ((q + 1) % 3 + 1) * ((q + 3) // 4)

    def dev(rr, qq):
        return (rr, qq)

    def at_q(xx, yy, cc):
        return xx * 8 + yy * 2 + cc

    def plane(off):
        return (r + off + NZ) % NZ

    def rcopy(src, dst, ssem, rsem, where):
        return pltpu.make_async_remote_copy(
            src_ref=src, dst_ref=dst, send_sem=ssem, recv_sem=rsem,
            device_id=where, device_id_type=pl.DeviceIdType.MESH)

    def got(dst, ssem, rsem, where):
        rcopy(dst, dst, ssem, rsem, where).wait_recv()

    def sent(src, ssem, rsem, where):
        rcopy(src, src, ssem, rsem, where).wait_send()

    x_up, x_dn = at_q((x + 1) % 4, y, core), at_q((x + 3) % 4, y, core)
    y_up, y_dn = at_q(x, (y + 1) % 4, core), at_q(x, (y + 3) % 4, core)
    mate = at_q(x, y, 1 - core)

    barrier = pltpu.get_barrier_semaphore()

    def greet(where):
        pl.semaphore_signal(barrier, inc=1, device_id=where, device_id_type=pl.DeviceIdType.MESH)

    for off in range(1, NZ):
        greet(dev(plane(off), q))
    for other in (x_up, x_dn, y_up, y_dn, mate):
        greet(dev(r, other))

    keeps = (q == 0) | (q == 2)
    gives = (q == 1) | (q == 3)

    @pl.when(jnp.logical_not(keeps))
    def _():
        greet(dev(r, p))

    @pl.when(gives)
    def _():
        greet(dev(r, at_q(0, home_y, 0)))

    @pl.when(q < 4)
    def _():
        for t in range(1, 8):
            greet(dev(r, at_q(t % 4, home_y, t // 4)))

    def colb(row):
        return jnp.transpose(jnp.broadcast_to(row, (128, 128)))

    pts = []
    for s in range(4):
        row = piv_ref[s:s + 1, :].astype(F32)
        pts.append(jnp.concatenate([colb(row[:, :128]), colb(row[:, 128:])], axis=0))
    sub = lax.broadcasted_iota(jnp.int32, (NB, 128), 0).astype(F32)
    lane = lax.broadcasted_iota(jnp.int32, (1, 128), 1).astype(F32)

    def swap(cur, s):
        target = sub + float(s * NB)
        delta = pts[s] - target
        move = jnp.where(target == cur, delta, 0.0) - jnp.where(pts[s] == cur, delta, 0.0)
        return cur + jnp.sum(move, axis=0, keepdims=True)

    def perm_tile(t, carry):
        start = lane + (t * 128).astype(F32)
        cur = start
        for s in (3, 2, 1, 0):
            cur = swap(cur, s)
        srcb[pl.ds(pl.multiple_of(t * 128, 128), 128), :] = colb(cur)
        cur = start
        for s in (0, 1, 2, 3):
            cur = swap(cur, s)
        destr[t] = cur
        return carry

    lax.fori_loop(0, 8, perm_tile, 0)

    @pl.when(keeps)
    def _():
        pl.semaphore_wait(barrier, 19)

    @pl.when(gives)
    def _():
        pl.semaphore_wait(barrier, 21)

    @pl.when(q >= 4)
    def _():
        pl.semaphore_wait(barrier, 13)

    def scatter_raw(t):
        tx_, tc = t % 4, t // 4
        return rcopy(a_ref.at[:, pl.ds(32 * t, 32), pl.ds(0, NB)],
                     pan.at[pl.ds(0, 8), pl.ds(32 * t, 32), pl.ds(pl.multiple_of(NB * q, NB), NB)],
                     sem_sc.at[t], rem_sc.at[0], dev(r, at_q(tx_, home_y, tc)))

    def raw_self():
        return pltpu.make_async_copy(a_ref.at[:, pl.ds(0, 32), pl.ds(0, NB)],
                                     pan.at[pl.ds(0, 8), pl.ds(0, 32), pl.ds(pl.multiple_of(NB * q, NB), NB)],
                                     loc_sem.at[0])

    @pl.when(keeps)
    def _():
        raw_self().start()

    @pl.when(gives)
    def _():
        scatter_raw(0).start()

    @pl.when(q < 4)
    def _():
        for t in range(1, 8):
            scatter_raw(t).start()

    def mirror():
        return rcopy(a_ref.at[0, pl.ds(128, 128), :],
                     old_own.at[r % 4, pl.ds(128, 128), :],
                     sem_mir.at[0], rem_mir.at[0], dev(7 - r, q))

    def old_self():
        return pltpu.make_async_copy(a_ref.at[0, pl.ds(0, 128), :],
                                     old_own.at[r % 4, pl.ds(0, 128), :], loc_sem.at[1])

    @pl.when(r < 4)
    def _():
        mirror().start()
        old_self().start()

    def contribute(i, carry):
        off = 4 + (i % 2) * ((i + 1) // 2) - (1 - i % 2) * (i // 2)
        chunk = (r + off) % NZ
        want = srcb[pl.ds(pl.multiple_of(chunk * 128, 128), 128), :]
        tiles = []
        for t in range(16):
            gid = lane + ((t // 2 * NZ + r) * NB + (t % 2) * 128).astype(F32)
            tiles.append(jnp.where(want == gid, 1.0, 0.0).astype(BF))
        pick = jnp.concatenate(tiles, axis=1)
        contrib[chunk] = dot(pick, a_ref[...].reshape(2048, COLS)).astype(BF)
        return carry

    def half(h):
        return pl.ds(NB * h, NB)

    def delta(h):
        return 1 if h == 0 else -1

    def rs_send(h, way, k):
        d = delta(h) if way == 0 else -delta(h)
        buf = rs_long if way == 0 else rs_short
        first = 4 if way == 0 else 3
        src = contrib.at[plane(first * d), :, half(h)] if k == 0 else buf.at[h, k - 1]
        idx = h * 7 + way * 4 + k
        return rcopy(src, buf.at[h, k], sem_rs.at[idx], rem_rs.at[idx], dev(plane(d), q))

    def rs_step(h, way, k):
        d = delta(h) if way == 0 else -delta(h)
        buf = rs_long if way == 0 else rs_short
        first = 4 if way == 0 else 3
        rs_send(h, way, k - 1).wait_recv()
        buf[h, k - 1] = buf[h, k - 1] + contrib[plane((first - k) * d), :, NB * h:NB * (h + 1)]
        rs_send(h, way, k).start()

    def rs_end(h):
        rs_send(h, 0, 3).wait_recv()
        rs_send(h, 1, 2).wait_recv()
        top_own[r, :, NB * h:NB * (h + 1)] = (
            contrib[r, :, NB * h:NB * (h + 1)] + rs_long[h, 3] + rs_short[h, 2])

    def top_view(j, h):
        return top_own.at[j, :, half(h)]

    def old_view(j, h):
        hi = j // 4
        a = j + hi * (7 - 2 * j)
        return old_own.at[a, pl.ds(pl.multiple_of(128 * hi, 128), 128), half(h)]

    def zag(view, ssem, rsem, h, way, k):
        d = delta(h) if way == 0 else -delta(h)
        idx = h * 7 + way * 4 + k
        v = view(plane(-k * d), h)
        return rcopy(v, v, ssem.at[idx], rsem.at[idx], dev(plane(d), q))

    def zag_got(view, ssem, rsem, h, way, k):
        d = delta(h) if way == 0 else -delta(h)
        idx = h * 7 + way * 4 + k
        got(view(plane(-(k + 1) * d), h), ssem.at[idx], rsem.at[idx], dev(plane(d), q))

    def zag_step(view, ssem, rsem, h, k):
        for way in range(2):
            if k < 4 - way:
                if k > 0:
                    zag_got(view, ssem, rsem, h, way, k - 1)
                zag(view, ssem, rsem, h, way, k).start()

    def zag_end(view, ssem, rsem, h):
        zag_got(view, ssem, rsem, h, 0, 3)
        zag_got(view, ssem, rsem, h, 1, 2)

    top_z = (top_view, sem_tz, rem_tz)
    old_z = (old_view, sem_dz, rem_dz)

    class Ring:
        def __init__(self, buf, n0, rows, base):
            self.buf, self.n0, self.rows, self.base = buf, n0, rows, base

        def reg(self, part, stage, j, piece=None):
            n0, rows = self.n0, self.rows
            lo, n = (0, n0 // 2) if part == 0 else (n0 // 2, n0 // 2)
            if piece is not None:
                n = n // 2
                lo = lo + n * piece
            k = pl.ds(lo, n)
            along_y = (part == 0) == (stage == 0)
            if stage == 0:
                col = panel_of(j) if along_y else p
                gg = g if along_y else core * 4 + j
                return self.buf.at[k, pl.ds(pl.multiple_of(rows * gg, rows), rows),
                                   pl.ds(pl.multiple_of(NB * col, NB), NB)]
            if part == 0:
                gg = core * 4 + j
                return self.buf.at[k, pl.ds(pl.multiple_of(rows * gg, rows), rows), :]
            return self.buf.at[k, pl.ds(pl.multiple_of(4 * rows * core, 4 * rows), 4 * rows),
                               pl.ds(pl.multiple_of(NB * panel_of(j), NB), NB)]

        def copy(self, part, stage, which):
            along_y = (part == 0) == (stage == 0)
            m = y if along_y else x
            up, dn = (y_up, y_dn) if along_y else (x_up, x_dn)
            idx = self.base + (part * 2 + stage) * 4 + which
            if which < 2:
                v = self.reg(part, stage, m)
            elif which == 2:
                v = self.reg(part, stage, (m + 3) % 4, 0)
            else:
                v = self.reg(part, stage, (m + 1) % 4, 1)
            return rcopy(v, v, sem_ring.at[idx], rem_ring.at[idx], dev(r, up if which % 2 == 0 else dn))

        def wait(self, part, stage, which):
            along_y = (part == 0) == (stage == 0)
            m = y if along_y else x
            idx = self.base + (part * 2 + stage) * 4 + which
            if which == 0:
                v = self.reg(part, stage, (m + 3) % 4)
            elif which == 1:
                v = self.reg(part, stage, (m + 1) % 4)
            else:
                v = self.reg(part, stage, (m + 2) % 4, which - 2)
            got(v, sem_ring.at[idx], rem_ring.at[idx], dev(r, mate))

        def par_view(self, part, piece):
            along_y = part == 1
            m = y if along_y else x
            return m, (0, 3, 1, 2)[piece]

        def par(self, part, piece):
            m, o = self.par_view(part, piece)
            v = self.reg(part, 1, (m + o) % 4)
            idx = self.base // 2 + part * 4 + piece
            return rcopy(v, v, sem_par.at[idx], rem_par.at[idx], dev(r, mate))

        def par_wait(self, part, piece):
            m, o = self.par_view(part, piece)
            v = self.reg_other(part, (m + o) % 4)
            idx = self.base // 2 + part * 4 + piece
            got(v, sem_par.at[idx], rem_par.at[idx], dev(r, mate))

        def reg_other(self, part, j):
            n0, rows = self.n0, self.rows
            oc = 1 - core
            if part == 0:
                gg = oc * 4 + j
                return self.buf.at[pl.ds(0, n0 // 2), pl.ds(pl.multiple_of(rows * gg, rows), rows), :]
            return self.buf.at[pl.ds(n0 // 2, n0 // 2),
                               pl.ds(pl.multiple_of(4 * rows * oc, 4 * rows), 4 * rows),
                               pl.ds(pl.multiple_of(NB * panel_of(j), NB), NB)]

        def start(self, stage):
            for part in range(2):
                self.copy(part, stage, 0).start()
                self.copy(part, stage, 1).start()

        def forward(self, stage):
            for part in range(2):
                self.wait(part, stage, 0)
                self.copy(part, stage, 2).start()
                self.wait(part, stage, 1)
                self.copy(part, stage, 3).start()
                if stage == 1:
                    self.par(part, 1).start()
                    self.par(part, 2).start()

        def finish(self, stage):
            for part in range(2):
                self.wait(part, stage, 2)
                self.wait(part, stage, 3)
                self.par(part, 0 if stage == 0 else 3).start()

        def close(self):
            for part in range(2):
                for piece in range(4):
                    self.par_wait(part, piece)

        def drain(self):
            for part in range(2):
                for stage in range(2):
                    for which in range(4):
                        self.copy(part, stage, which).wait_send()
                for piece in range(4):
                    self.par(part, piece).wait_send()

    ring_raw = Ring(pan, 12, 32, 0)
    ring_top = Ring(top_pan, 8, 16, 16)

    mine32 = pl.ds(pl.multiple_of(32 * g, 32), 32)
    mine16 = pl.ds(pl.multiple_of(16 * g, 16), 16)
    minec = pl.ds(pl.multiple_of(NB * p, NB), NB)

    def old_slice(off):
        return rcopy(pan.at[0, mine32, minec], pan.at[8 + r % 4, mine32, minec],
                     sem_ds.at[off - 1], rem_ds.at[r % 4], dev(plane(off), q))

    def old_slice_self():
        return pltpu.make_async_copy(pan.at[0, mine32, minec], pan.at[8 + r % 4, mine32, minec],
                                     loc_sem.at[2])

    def top_piece(t):
        return rcopy(top_own.at[r, pl.ds(16 * t, 16), pl.ds(0, NB)],
                     top_pan.at[r, pl.ds(16 * t, 16), pl.ds(pl.multiple_of(NB * q, NB), NB)],
                     sem_ts.at[t], rem_ts.at[0], dev(r, at_q(t % 4, home_y, t // 4)))

    def top_piece_self():
        return pltpu.make_async_copy(top_own.at[r, pl.ds(0, 16), pl.ds(0, NB)],
                                     top_pan.at[r, pl.ds(0, 16), pl.ds(pl.multiple_of(NB * q, NB), NB)],
                                     loc_sem.at[3])

    def top_slice(off):
        v = top_pan.at[r, mine16, minec]
        return rcopy(v, v, sem_tsl.at[off - 1], rem_tsl.at[r], dev(plane(off), q))

    lax.fori_loop(0, 3, contribute, 0)
    for h in range(2):
        rs_send(h, 0, 0).start()
        rs_send(h, 1, 0).start()
    lax.fori_loop(3, 8, contribute, 0)

    for h in range(2):
        rs_step(h, 0, 1)
        rs_step(h, 1, 1)

    @pl.when(keeps)
    def _():
        raw_self().wait()

    @pl.when(jnp.logical_not(keeps))
    def _():
        got(pan.at[pl.ds(0, 8), mine32, minec], sem_sc.at[0], rem_sc.at[0], dev(r, mate))

    @pl.when(r < 4)
    def _():
        old_slice_self().start()
        for off in range(1, NZ):
            old_slice(off).start()
        old_self().wait()

    @pl.when(r >= 4)
    def _():
        got(old_own.at[(7 - r) % 4, pl.ds(128, 128), :], sem_mir.at[0], rem_mir.at[0], dev(7 - r, q))

    for h in range(2):
        rs_step(h, 0, 2)
        rs_step(h, 1, 2)

    for h in range(2):
        zag_step(*old_z, h, 0)

    for a in range(4):
        @pl.when(r != a)
        def _():
            got(pan.at[8 + a, mine32, minec], sem_ds.at[0], rem_ds.at[a], dev(r, mate))

    @pl.when(r < 4)
    def _():
        old_slice_self().wait()

    ring_raw.start(0)

    for h in range(2):
        rs_step(h, 0, 3)

    rs_end(0)

    @pl.when(keeps)
    def _():
        top_piece_self().start()

    @pl.when(gives)
    def _():
        top_piece(0).start()

    @pl.when(q < 4)
    def _():
        for t in range(1, 8):
            top_piece(t).start()

    zag_step(*top_z, 0, 0)
    rs_end(1)
    zag_step(*top_z, 1, 0)

    for h in range(2):
        zag_step(*old_z, h, 1)

    ring_raw.forward(0)

    @pl.when(keeps)
    def _():
        top_piece_self().wait()

    @pl.when(jnp.logical_not(keeps))
    def _():
        got(top_pan.at[r, mine16, minec], sem_ts.at[0], rem_ts.at[0], dev(r, mate))

    for off in range(1, NZ):
        top_slice(off).start()

    for h in range(2):
        zag_step(*top_z, h, 1)
    for h in range(2):
        zag_step(*old_z, h, 2)

    for off in range(1, NZ):
        src = plane(off)
        got(top_pan.at[src, mine16, minec], sem_tsl.at[0], rem_tsl.at[src], dev(r, mate))

    ring_top.start(0)
    ring_raw.finish(0)
    ring_raw.start(1)

    for h in range(2):
        zag_step(*top_z, h, 2)
    for h in range(2):
        zag_step(*old_z, h, 3)

    ring_top.forward(0)
    ring_top.finish(0)
    ring_top.start(1)

    for h in range(2):
        zag_step(*top_z, h, 3)

    ring_raw.forward(1)
    ring_top.forward(1)
    for h in range(2):
        zag_end(*old_z, h)
        zag_end(*top_z, h)
    ring_raw.finish(1)
    ring_raw.close()

    row_id = lax.broadcasted_iota(jnp.int32, (NB, 1), 0).astype(F32)

    def displaced(k, carry):
        mine = row_id + ((k * NZ + r) * NB).astype(F32)
        tiles, seen = [], None
        for t in range(8):
            hit = jnp.where(destr[t] == mine, 1.0, 0.0)
            seen = hit if seen is None else seen + hit
            tiles.append(hit.astype(BF))
        pick = jnp.concatenate(tiles, axis=1)
        moved = jnp.sum(seen, axis=1, keepdims=True) > 0.5
        rows = dot(pick, pan[8:12].reshape(TOP, TOP))
        left[k] = jnp.where(moved, rows, pan[k].astype(F32)).astype(BF)
        rows = dot(pick, old_own[...].reshape(TOP, COLS))
        out_ref[k] = jnp.where(moved, rows, a_ref[k].astype(F32)).astype(BF)
        return carry

    lax.fori_loop(0, 8, displaced, 0)

    ring_top.finish(1)
    ring_top.close()

    tx[...] = top_pan[...].reshape(TOP, TOP)
    ux[...] = top_own[...].reshape(TOP, COLS)
    for s in range(4):
        b, e = s * NB, (s + 1) * NB
        u_own = dot(linv_ref[s], ux[b:e, :]).astype(BF)
        ux[b:e, :] = u_own
        if s < 3:
            l_top = dot(tx[e:, b:e], uinv_ref[s]).astype(BF)
            tx[e:, b:e] = l_top
            u_pan = dot(linv_ref[s], tx[b:e, e:]).astype(BF)
            tx[b:e, e:] = u_pan
            tx[e:, e:] = (tx[e:, e:].astype(F32) - dot(l_top, u_pan)).astype(BF)
            ux[e:, :] = (ux[e:, :].astype(F32) - dot(l_top, u_own)).astype(BF)

    mycol = pl.ds(pl.multiple_of(NB * jnp.minimum(q, 3), NB), NB)

    def below(k, carry):
        for s in range(4):
            b, e = s * NB, (s + 1) * NB
            l_row = dot(left[k, :, b:e], uinv_ref[s]).astype(BF)
            left[k, :, b:e] = l_row
            if s < 3:
                left[k, :, e:] = (left[k, :, e:].astype(F32) - dot(l_row, tx[b:e, e:])).astype(BF)
        out_ref[k] = (out_ref[k].astype(F32) - dot(left[k], ux[...])).astype(BF)

        @pl.when(q < 4)
        def _():
            out_ref[k, :, 0:NB] = left[k, :, mycol]

        return carry

    lax.fori_loop(0, 8, below, 0)

    toprow = pl.ds(pl.multiple_of(NB * jnp.minimum(r, 3), NB), NB)

    @pl.when(r < 4)
    def _():
        out_ref[0] = ux[toprow, :]

        @pl.when(q < 4)
        def _():
            out_ref[0, :, 0:NB] = tx[toprow, mycol]

    @pl.when(gives)
    def _():
        scatter_raw(0).wait_send()
        top_piece(0).wait_send()

    @pl.when(q < 4)
    def _():
        for t in range(1, 8):
            scatter_raw(t).wait_send()
            top_piece(t).wait_send()

    @pl.when(r < 4)
    def _():
        mirror().wait_send()
        for off in range(1, NZ):
            old_slice(off).wait_send()

    for off in range(1, NZ):
        top_slice(off).wait_send()
    for h in range(2):
        for way in range(2):
            for k in range(4 - way):
                rs_send(h, way, k).wait_send()
                zag(*top_z, h, way, k).wait_send()
                zag(*old_z, h, way, k).wait_send()
    ring_raw.drain()
    ring_top.drain()


def local(matrix, pivots, lower_inverse, upper_inverse):
    a = matrix.reshape(8, NB, COLS)
    vm = pl.BlockSpec(memory_space=pltpu.VMEM)
    dma = pltpu.SemaphoreType.DMA
    out = pl.pallas_call(
        kernel,
        out_shape=jax.ShapeDtypeStruct((8, NB, COLS), BF),
        in_specs=[vm] * 4,
        out_specs=vm,
        scratch_shapes=[
            pltpu.VMEM((TOP, 128), F32),
            pltpu.VMEM((8, 1, 128), F32),
            pltpu.VMEM((8, 128, COLS), BF),
            pltpu.VMEM((2, 4, 128, NB), BF),
            pltpu.VMEM((2, 3, 128, NB), BF),
            pltpu.VMEM((8, 128, COLS), BF),
            pltpu.VMEM((4, NB, COLS), BF),
            pltpu.VMEM((12, NB, TOP), BF),
            pltpu.VMEM((8, 128, TOP), BF),
            pltpu.VMEM((8, NB, TOP), BF),
            pltpu.VMEM((TOP, TOP), BF),
            pltpu.VMEM((TOP, COLS), BF),
            dma((14,)), dma((14,)), dma((14,)), dma((14,)), dma((14,)), dma((14,)),
            dma((8,)), dma((1,)), dma((1,)), dma((1,)), dma((4,)), dma((7,)), dma((4,)),
            dma((8,)), dma((1,)), dma((7,)), dma((8,)),
            dma((32,)), dma((32,)), dma((16,)), dma((16,)),
        ],
        compiler_params=pltpu.CompilerParams(
            collective_id=0, has_side_effects=True, vmem_limit_bytes=60 * 1024 * 1024),
    )(a, pivots, lower_inverse, upper_inverse)
    return out.reshape(matrix.shape)


def solution(mesh):
    placed = (P(None, "prow", None, "pcol"), P(), P(), P())
    return jax.shard_map(
        local, mesh=mesh, in_specs=placed, out_specs=P(None, "prow", None, "pcol"), check_vma=False
    )
```

```python
import jax
import jax.numpy as jnp
from jax import lax
from jax.experimental import pallas as pl
from jax.experimental.pallas import tpu as pltpu
from jax.sharding import PartitionSpec as P

BF = jnp.bfloat16
F32 = jnp.float32
NB = 256
NZ = 8
TOP = 1024
COLS = 512


def dot(a, b):
    return jnp.dot(a, b, preferred_element_type=F32)


def kernel(a_ref, piv_ref, linv_ref, uinv_ref, out_ref,
           srcb, destr, contrib, rs_long, rs_short, top_own, old_own, pan, top_pan,
           left, tx, ux, pick, place, moved, piece_own, piece_rx,
           sem_rs, rem_rs, sem_tz, rem_tz, sem_dz, rem_dz,
           sem_sc, rem_sc, sem_mir, rem_mir, loc_sem, sem_ds, rem_ds,
           sem_ts, rem_ts, sem_px, rem_px, sem_tsl, rem_tsl,
           sem_ring, rem_ring, sem_par, rem_par):
    r = lax.axis_index("prow")
    q = lax.axis_index("pcol")
    x = q // 8
    y = (q // 2) % 4
    core = q % 2
    g = core * 4 + x

    def panel_of(yy):
        return (yy % 3 + 1) * ((yy + 3) // 4)

    p = panel_of(y)
    home_y = ((q + 1) % 3 + 1) * ((q + 3) // 4)

    def dev(rr, qq):
        return (rr, qq)

    def at_q(xx, yy, cc):
        return xx * 8 + yy * 2 + cc

    def plane(off):
        return (r + off + NZ) % NZ

    def rcopy(src, dst, ssem, rsem, where):
        return pltpu.make_async_remote_copy(
            src_ref=src, dst_ref=dst, send_sem=ssem, recv_sem=rsem,
            device_id=where, device_id_type=pl.DeviceIdType.MESH)

    def got(dst, ssem, rsem, where):
        rcopy(dst, dst, ssem, rsem, where).wait_recv()

    def sent(src, ssem, rsem, where):
        rcopy(src, src, ssem, rsem, where).wait_send()

    x_up, x_dn = at_q((x + 1) % 4, y, core), at_q((x + 3) % 4, y, core)
    y_up, y_dn = at_q(x, (y + 1) % 4, core), at_q(x, (y + 3) % 4, core)
    mate = at_q(x, y, 1 - core)

    barrier = pltpu.get_barrier_semaphore()

    def greet(where):
        pl.semaphore_signal(barrier, inc=1, device_id=where, device_id_type=pl.DeviceIdType.MESH)

    for off in range(1, NZ):
        greet(dev(plane(off), q))
    for other in (x_up, x_dn, y_up, y_dn, mate):
        greet(dev(r, other))

    keeps = (q == 0) | (q == 2)
    gives = (q == 1) | (q == 3)

    @pl.when(jnp.logical_not(keeps))
    def _():
        greet(dev(r, p))

    @pl.when(gives)
    def _():
        greet(dev(r, at_q(0, home_y, 0)))

    @pl.when(q < 4)
    def _():
        for t in range(1, 8):
            greet(dev(r, at_q(t % 4, home_y, t // 4)))

    def colb(row):
        return jnp.transpose(jnp.broadcast_to(row, (128, 128)))

    pts = []
    for s in range(4):
        row = piv_ref[s:s + 1, :].astype(F32)
        pts.append(jnp.concatenate([colb(row[:, :128]), colb(row[:, 128:])], axis=0))
    sub = lax.broadcasted_iota(jnp.int32, (NB, 128), 0).astype(F32)
    lane = lax.broadcasted_iota(jnp.int32, (1, 128), 1).astype(F32)

    def swap(cur, s):
        target = sub + float(s * NB)
        delta = pts[s] - target
        move = jnp.where(target == cur, delta, 0.0) - jnp.where(pts[s] == cur, delta, 0.0)
        return cur + jnp.sum(move, axis=0, keepdims=True)

    def perm_tile(t, carry):
        start = lane + (t * 128).astype(F32)
        cur = start
        for s in (3, 2, 1, 0):
            cur = swap(cur, s)
        srcb[pl.ds(pl.multiple_of(t * 128, 128), 128), :] = colb(cur)
        cur = start
        for s in (0, 1, 2, 3):
            cur = swap(cur, s)
        destr[t] = cur
        return carry

    lax.fori_loop(0, 8, perm_tile, 0)

    @pl.when(keeps)
    def _():
        pl.semaphore_wait(barrier, 19)

    @pl.when(gives)
    def _():
        pl.semaphore_wait(barrier, 21)

    @pl.when(q >= 4)
    def _():
        pl.semaphore_wait(barrier, 13)

    groups = ((0, 2), (2, 4), (6, 2))

    def scatter_raw(t, n):
        lo, size = groups[n]
        return rcopy(a_ref.at[pl.ds(lo, size), pl.ds(32 * t, 32), pl.ds(0, NB)],
                     pan.at[pl.ds(lo, size), pl.ds(32 * t, 32), pl.ds(pl.multiple_of(NB * q, NB), NB)],
                     sem_sc.at[8 * n + t], rem_sc.at[n], dev(r, at_q(t % 4, home_y, t // 4)))

    def raw_self(n):
        lo, size = groups[n]
        return pltpu.make_async_copy(
            a_ref.at[pl.ds(lo, size), pl.ds(0, 32), pl.ds(0, NB)],
            pan.at[pl.ds(lo, size), pl.ds(0, 32), pl.ds(pl.multiple_of(NB * q, NB), NB)],
            loc_sem.at[3 + n])

    def raw_start(n):
        @pl.when(keeps)
        def _():
            raw_self(n).start()

        @pl.when(gives)
        def _():
            scatter_raw(0, n).start()

        @pl.when(q < 4)
        def _():
            for t in range(1, 8):
                scatter_raw(t, n).start()

    def raw_wait(n):
        lo, size = groups[n]

        @pl.when(keeps)
        def _():
            raw_self(n).wait()

        @pl.when(jnp.logical_not(keeps))
        def _():
            got(pan.at[pl.ds(lo, size), mine32, minec], sem_sc.at[0], rem_sc.at[n], dev(r, mate))

    def mirror():
        return rcopy(a_ref.at[0, pl.ds(128, 128), :],
                     old_own.at[r % 4, pl.ds(128, 128), :],
                     sem_mir.at[0], rem_mir.at[0], dev(7 - r, q))

    def old_self():
        return pltpu.make_async_copy(a_ref.at[0, pl.ds(0, 128), :],
                                     old_own.at[r % 4, pl.ds(0, 128), :], loc_sem.at[1])

    def contribute(h):
        def body(c, carry):
            if h == 0:
                want = srcb[pl.ds(pl.multiple_of(c * 128, 128), 128), :]
                for t in range(16):
                    gid = lane + ((t // 2 * NZ + r) * NB + (t % 2) * 128).astype(F32)
                    pick[c, :, 128 * t:128 * (t + 1)] = jnp.where(want == gid, 1.0, 0.0).astype(BF)
            contrib[c, :, NB * h:NB * (h + 1)] = dot(
                pick[c], a_ref[:, :, NB * h:NB * (h + 1)].reshape(2048, NB)).astype(BF)
            return carry

        lax.fori_loop(0, 8, body, 0)

    def half(h):
        return pl.ds(NB * h, NB)

    def delta(h):
        return 1 if h == 0 else -1

    def rs_send(h, way, k):
        d = delta(h) if way == 0 else -delta(h)
        buf = rs_long if way == 0 else rs_short
        first = 4 if way == 0 else 3
        src = contrib.at[plane(first * d), :, half(h)] if k == 0 else buf.at[h, k - 1]
        idx = h * 7 + way * 4 + k
        return rcopy(src, buf.at[h, k], sem_rs.at[idx], rem_rs.at[idx], dev(plane(d), q))

    def rs_step(h, way, k):
        d = delta(h) if way == 0 else -delta(h)
        buf = rs_long if way == 0 else rs_short
        first = 4 if way == 0 else 3
        rs_send(h, way, k - 1).wait_recv()
        buf[h, k - 1] = buf[h, k - 1] + contrib[plane((first - k) * d), :, NB * h:NB * (h + 1)]
        rs_send(h, way, k).start()

    def rs_end(h):
        rs_send(h, 0, 3).wait_recv()
        rs_send(h, 1, 2).wait_recv()
        top_own[r, :, NB * h:NB * (h + 1)] = (
            contrib[r, :, NB * h:NB * (h + 1)] + rs_long[h, 3] + rs_short[h, 2])

    def top_view(j, h):
        return top_own.at[j, :, half(h)]

    def old_view(j, h):
        hi = j // 4
        a = j + hi * (7 - 2 * j)
        return old_own.at[a, pl.ds(pl.multiple_of(128 * hi, 128), 128), half(h)]

    def zag(view, ssem, rsem, h, way, k):
        d = delta(h) if way == 0 else -delta(h)
        idx = h * 7 + way * 4 + k
        v = view(plane(-k * d), h)
        return rcopy(v, v, ssem.at[idx], rsem.at[idx], dev(plane(d), q))

    def zag_got(view, ssem, rsem, h, way, k):
        d = delta(h) if way == 0 else -delta(h)
        idx = h * 7 + way * 4 + k
        got(view(plane(-(k + 1) * d), h), ssem.at[idx], rsem.at[idx], dev(plane(d), q))

    def zag_step(view, ssem, rsem, h, k):
        for way in range(2):
            if k < 4 - way:
                if k > 0:
                    zag_got(view, ssem, rsem, h, way, k - 1)
                zag(view, ssem, rsem, h, way, k).start()

    def zag_end(view, ssem, rsem, h):
        zag_got(view, ssem, rsem, h, 0, 3)
        zag_got(view, ssem, rsem, h, 1, 2)

    top_z = (top_view, sem_tz, rem_tz)
    old_z = (old_view, sem_dz, rem_dz)

    class Ring:
        def __init__(self, buf, n0, rows, base):
            self.buf, self.n0, self.rows, self.base = buf, n0, rows, base

        def reg(self, part, stage, j, piece=None):
            n0, rows = self.n0, self.rows
            lo, n = (0, n0 // 2) if part == 0 else (n0 // 2, n0 // 2)
            if piece is not None:
                n = n // 2
                lo = lo + n * piece
            k = pl.ds(lo, n)
            along_y = (part == 0) == (stage == 0)
            if stage == 0:
                col = panel_of(j) if along_y else p
                gg = g if along_y else core * 4 + j
                return self.buf.at[k, pl.ds(pl.multiple_of(rows * gg, rows), rows),
                                   pl.ds(pl.multiple_of(NB * col, NB), NB)]
            if part == 0:
                gg = core * 4 + j
                return self.buf.at[k, pl.ds(pl.multiple_of(rows * gg, rows), rows), :]
            return self.buf.at[k, pl.ds(pl.multiple_of(4 * rows * core, 4 * rows), 4 * rows),
                               pl.ds(pl.multiple_of(NB * panel_of(j), NB), NB)]

        def copy(self, part, stage, which):
            along_y = (part == 0) == (stage == 0)
            m = y if along_y else x
            up, dn = (y_up, y_dn) if along_y else (x_up, x_dn)
            idx = self.base + (part * 2 + stage) * 4 + which
            if which < 2:
                v = self.reg(part, stage, m)
            elif which == 2:
                v = self.reg(part, stage, (m + 3) % 4, 0)
            else:
                v = self.reg(part, stage, (m + 1) % 4, 1)
            return rcopy(v, v, sem_ring.at[idx], rem_ring.at[idx], dev(r, up if which % 2 == 0 else dn))

        def wait(self, part, stage, which):
            along_y = (part == 0) == (stage == 0)
            m = y if along_y else x
            idx = self.base + (part * 2 + stage) * 4 + which
            if which == 0:
                v = self.reg(part, stage, (m + 3) % 4)
            elif which == 1:
                v = self.reg(part, stage, (m + 1) % 4)
            else:
                v = self.reg(part, stage, (m + 2) % 4, which - 2)
            got(v, sem_ring.at[idx], rem_ring.at[idx], dev(r, mate))

        def par_view(self, part, piece):
            along_y = part == 1
            m = y if along_y else x
            return m, (0, 3, 1, 2)[piece]

        def par(self, part, piece):
            m, o = self.par_view(part, piece)
            v = self.reg(part, 1, (m + o) % 4)
            idx = self.base // 2 + part * 4 + piece
            return rcopy(v, v, sem_par.at[idx], rem_par.at[idx], dev(r, mate))

        def par_wait(self, part, piece):
            m, o = self.par_view(part, piece)
            v = self.reg_other(part, (m + o) % 4)
            idx = self.base // 2 + part * 4 + piece
            got(v, sem_par.at[idx], rem_par.at[idx], dev(r, mate))

        def reg_other(self, part, j):
            n0, rows = self.n0, self.rows
            oc = 1 - core
            if part == 0:
                gg = oc * 4 + j
                return self.buf.at[pl.ds(0, n0 // 2), pl.ds(pl.multiple_of(rows * gg, rows), rows), :]
            return self.buf.at[pl.ds(n0 // 2, n0 // 2),
                               pl.ds(pl.multiple_of(4 * rows * oc, 4 * rows), 4 * rows),
                               pl.ds(pl.multiple_of(NB * panel_of(j), NB), NB)]

        def start(self, stage, parts=(0, 1)):
            for part in parts:
                self.copy(part, stage, 0).start()
                self.copy(part, stage, 1).start()

        def forward(self, stage):
            for part in range(2):
                self.wait(part, stage, 0)
                self.copy(part, stage, 2).start()
                self.wait(part, stage, 1)
                self.copy(part, stage, 3).start()
                if stage == 1:
                    self.par(part, 1).start()
                    self.par(part, 2).start()

        def finish(self, stage):
            for part in range(2):
                self.wait(part, stage, 2)
                self.wait(part, stage, 3)
                self.par(part, 0 if stage == 0 else 3).start()

        def close(self):
            for part in range(2):
                for piece in range(4):
                    self.par_wait(part, piece)

        def drain(self):
            for part in range(2):
                for stage in range(2):
                    for which in range(4):
                        self.copy(part, stage, which).wait_send()
                for piece in range(4):
                    self.par(part, piece).wait_send()

    ring_raw = Ring(pan, 12, 32, 0)
    ring_top = Ring(top_pan, 8, 16, 16)

    mine32 = pl.ds(pl.multiple_of(32 * g, 32), 32)
    mine16 = pl.ds(pl.multiple_of(16 * g, 16), 16)
    minec = pl.ds(pl.multiple_of(NB * p, NB), NB)

    def old_slice(off):
        return rcopy(pan.at[0, mine32, minec], pan.at[8 + r % 4, mine32, minec],
                     sem_ds.at[off - 1], rem_ds.at[r % 4], dev(plane(off), q))

    def old_slice_self():
        return pltpu.make_async_copy(pan.at[0, mine32, minec], pan.at[8 + r % 4, mine32, minec],
                                     loc_sem.at[0])

    def top_piece(t):
        return rcopy(contrib.at[:, pl.ds(16 * t, 16), pl.ds(0, NB)], piece_own,
                     sem_ts.at[t], rem_ts.at[0], dev(r, at_q(t % 4, home_y, t // 4)))

    def top_piece_self():
        return pltpu.make_async_copy(contrib.at[:, pl.ds(0, 16), pl.ds(0, NB)], piece_own, loc_sem.at[2])

    def piece_home(off):
        return rcopy(piece_own.at[plane(off)], piece_rx.at[r], sem_px.at[off - 1], rem_px.at[r],
                     dev(plane(off), q))

    def top_slice(off):
        v = top_pan.at[r, mine16, minec]
        return rcopy(v, v, sem_tsl.at[off - 1], rem_tsl.at[r], dev(plane(off), q))

    row_id = lax.broadcasted_iota(jnp.int32, (NB, 1), 0).astype(F32)

    def displaced_own(k, carry):
        mine = row_id + ((k * NZ + r) * NB).astype(F32)
        seen = None
        for t in range(8):
            hit = jnp.where(destr[t] == mine, 1.0, 0.0)
            seen = hit if seen is None else seen + hit
            place[k, :, 128 * t:128 * (t + 1)] = hit.astype(BF)
        some = jnp.sum(seen, axis=1, keepdims=True)
        moved[k] = jnp.broadcast_to(some, (NB, 128))
        rows = dot(place[k], old_own[...].reshape(TOP, COLS))
        out_ref[k] = jnp.where(some > 0.5, rows, a_ref[k].astype(F32)).astype(BF)
        return carry

    def displaced_panel(k, carry):
        rows = dot(place[k], pan[8:12].reshape(TOP, TOP))
        left[k] = jnp.where(moved[k][:, 0:1] > 0.5, rows, pan[k].astype(F32)).astype(BF)
        return carry

    raw_start(0)

    @pl.when(r < 4)
    def _():
        mirror().start()
        old_self().start()

    contribute(0)

    @pl.when(keeps)
    def _():
        top_piece_self().start()

    @pl.when(gives)
    def _():
        top_piece(0).start()

    @pl.when(q < 4)
    def _():
        for t in range(1, 8):
            top_piece(t).start()

    rs_send(0, 0, 0).start()
    rs_send(0, 1, 0).start()
    raw_start(1)
    raw_start(2)
    contribute(1)
    rs_send(1, 0, 0).start()
    rs_send(1, 1, 0).start()

    @pl.when(r < 4)
    def _():
        old_self().wait()

    @pl.when(r >= 4)
    def _():
        got(old_own.at[(7 - r) % 4, pl.ds(128, 128), :], sem_mir.at[0], rem_mir.at[0], dev(7 - r, q))

    for h in range(2):
        zag_step(*old_z, h, 0)

    raw_wait(0)

    @pl.when(r < 4)
    def _():
        old_slice_self().start()
        for off in range(1, NZ):
            old_slice(off).start()

    for h in range(2):
        rs_step(h, 0, 1)
        rs_step(h, 1, 1)

    @pl.when(keeps)
    def _():
        top_piece_self().wait()

    @pl.when(jnp.logical_not(keeps))
    def _():
        got(piece_own, sem_ts.at[0], rem_ts.at[0], dev(r, mate))

    for off in range(1, NZ):
        piece_home(off).start()

    for h in range(2):
        zag_step(*old_z, h, 1)

    for h in range(2):
        rs_step(h, 0, 2)
        rs_step(h, 1, 2)

    total = piece_own[r]
    for off in range(1, NZ):
        src = plane(off)
        got(piece_rx.at[src], sem_px.at[0], rem_px.at[src], dev(r, mate))
        total = total + piece_rx[src]
    top_pan[r, mine16, minec] = total
    for off in range(1, NZ):
        top_slice(off).start()

    raw_wait(1)
    ring_raw.start(0, (0,))

    for a in range(4):
        @pl.when(r != a)
        def _():
            got(pan.at[8 + a, mine32, minec], sem_ds.at[0], rem_ds.at[a], dev(r, mate))

    @pl.when(r < 4)
    def _():
        old_slice_self().wait()

    raw_wait(2)
    ring_raw.start(0, (1,))

    for h in range(2):
        rs_step(h, 0, 3)
        zag_step(*old_z, h, 2)

    for off in range(1, NZ):
        src = plane(off)
        got(top_pan.at[src, mine16, minec], sem_tsl.at[0], rem_tsl.at[src], dev(r, mate))

    ring_top.start(0)

    for h in range(2):
        rs_end(h)
        zag_step(*top_z, h, 0)
    for h in range(2):
        zag_step(*old_z, h, 3)

    ring_raw.forward(0)
    ring_top.forward(0)
    for h in range(2):
        zag_step(*top_z, h, 1)

    ring_raw.finish(0)
    ring_raw.start(1)
    ring_top.finish(0)
    ring_top.start(1)

    for h in range(2):
        zag_end(*old_z, h)
    for h in range(2):
        zag_step(*top_z, h, 2)

    lax.fori_loop(0, 8, displaced_own, 0)

    ring_raw.forward(1)
    ring_top.forward(1)
    for h in range(2):
        zag_step(*top_z, h, 3)

    ring_raw.finish(1)
    ring_raw.close()
    lax.fori_loop(0, 8, displaced_panel, 0)

    for h in range(2):
        zag_end(*top_z, h)
    ring_top.finish(1)
    ring_top.close()

    tx[...] = top_pan[...].reshape(TOP, TOP)
    ux[...] = top_own[...].reshape(TOP, COLS)
    for s in range(4):
        b, e = s * NB, (s + 1) * NB
        u_own = dot(linv_ref[s], ux[b:e, :]).astype(BF)
        ux[b:e, :] = u_own
        if s < 3:
            l_top = dot(tx[e:, b:e], uinv_ref[s]).astype(BF)
            tx[e:, b:e] = l_top
            u_pan = dot(linv_ref[s], tx[b:e, e:]).astype(BF)
            tx[b:e, e:] = u_pan
            tx[e:, e:] = (tx[e:, e:].astype(F32) - dot(l_top, u_pan)).astype(BF)
            ux[e:, :] = (ux[e:, :].astype(F32) - dot(l_top, u_own)).astype(BF)

    mycol = pl.ds(pl.multiple_of(NB * jnp.minimum(q, 3), NB), NB)

    TWO = 2

    def below(i, carry):
        ks = pl.ds(TWO * i, TWO)
        m = TWO * NB
        for s in range(4):
            b, e = s * NB, (s + 1) * NB
            l_row = dot(left[ks, :, b:e].reshape(m, NB), uinv_ref[s]).astype(BF)
            left[ks, :, b:e] = l_row.reshape(TWO, NB, NB)
            if s < 3:
                rest = left[ks, :, e:].reshape(m, TOP - e).astype(F32)
                left[ks, :, e:] = (rest - dot(l_row, tx[b:e, e:])).astype(BF).reshape(TWO, NB, TOP - e)
        rest = out_ref[ks].reshape(m, COLS).astype(F32)
        rest = rest - dot(left[ks].reshape(m, TOP), ux[...])
        out_ref[ks] = rest.astype(BF).reshape(TWO, NB, COLS)

        @pl.when(q < 4)
        def _():
            out_ref[ks, :, 0:NB] = left[ks, :, mycol]

        return carry

    lax.fori_loop(0, 8 // TWO, below, 0)

    toprow = pl.ds(pl.multiple_of(NB * jnp.minimum(r, 3), NB), NB)

    @pl.when(r < 4)
    def _():
        out_ref[0] = ux[toprow, :]

        @pl.when(q < 4)
        def _():
            out_ref[0, :, 0:NB] = tx[toprow, mycol]

    @pl.when(gives)
    def _():
        for n in range(3):
            scatter_raw(0, n).wait_send()
        top_piece(0).wait_send()

    @pl.when(q < 4)
    def _():
        for t in range(1, 8):
            for n in range(3):
                scatter_raw(t, n).wait_send()
            top_piece(t).wait_send()

    @pl.when(r < 4)
    def _():
        mirror().wait_send()
        for off in range(1, NZ):
            old_slice(off).wait_send()

    for off in range(1, NZ):
        piece_home(off).wait_send()
    for off in range(1, NZ):
        top_slice(off).wait_send()
    for h in range(2):
        for way in range(2):
            for k in range(4 - way):
                rs_send(h, way, k).wait_send()
                zag(*top_z, h, way, k).wait_send()
                zag(*old_z, h, way, k).wait_send()
    ring_raw.drain()
    ring_top.drain()


def local(matrix, pivots, lower_inverse, upper_inverse):
    rows = matrix.reshape(256, 8, 2, NB).transpose(0, 2, 1, 3)
    a = lax.optimization_barrier(rows).transpose(0, 2, 1, 3).reshape(8, NB, COLS)
    vm = pl.BlockSpec(memory_space=pltpu.VMEM)
    dma = pltpu.SemaphoreType.DMA
    out = pl.pallas_call(
        kernel,
        out_shape=jax.ShapeDtypeStruct((8, NB, COLS), BF),
        in_specs=[vm] * 4,
        out_specs=vm,
        scratch_shapes=[
            pltpu.VMEM((TOP, 128), F32),
            pltpu.VMEM((8, 1, 128), F32),
            pltpu.VMEM((8, 128, COLS), BF),
            pltpu.VMEM((2, 4, 128, NB), BF),
            pltpu.VMEM((2, 3, 128, NB), BF),
            pltpu.VMEM((8, 128, COLS), BF),
            pltpu.VMEM((4, NB, COLS), BF),
            pltpu.VMEM((12, NB, TOP), BF),
            pltpu.VMEM((8, 128, TOP), BF),
            pltpu.VMEM((8, NB, TOP), BF),
            pltpu.VMEM((TOP, TOP), BF),
            pltpu.VMEM((TOP, COLS), BF),
            pltpu.VMEM((8, 128, 2048), BF),
            pltpu.VMEM((8, NB, TOP), BF),
            pltpu.VMEM((8, NB, 128), F32),
            pltpu.VMEM((8, 16, NB), BF),
            pltpu.VMEM((8, 16, NB), BF),
            dma((14,)), dma((14,)), dma((14,)), dma((14,)), dma((14,)), dma((14,)),
            dma((24,)), dma((3,)), dma((1,)), dma((1,)), dma((6,)), dma((7,)), dma((4,)),
            dma((8,)), dma((1,)), dma((7,)), dma((8,)), dma((7,)), dma((8,)),
            dma((32,)), dma((32,)), dma((16,)), dma((16,)),
        ],
        compiler_params=pltpu.CompilerParams(
            collective_id=0, has_side_effects=True, vmem_limit_bytes=46 * 1024 * 1024),
    )(a, pivots, lower_inverse, upper_inverse)
    return out.reshape(matrix.shape)


def solution(mesh):
    placed = (P(None, "prow", None, "pcol"), P(), P(), P())
    return jax.shard_map(
        local, mesh=mesh, in_specs=placed, out_specs=P(None, "prow", None, "pcol"), check_vma=False
    )
```

```python
import jax
import jax.numpy as jnp
from jax import lax
from jax.experimental import pallas as pl
from jax.experimental.pallas import tpu as pltpu
from jax.sharding import PartitionSpec as P

BF = jnp.bfloat16
F32 = jnp.float32
NB = 256
NZ = 8
TOP = 1024
COLS = 512


ORDER = ('w0', 'w1', 'w2', 'os', 'C0', 'r00', 'C1', 'r10', 'g0', 'ls', 'r01', 'g1', 'R00s', 'P', 'r11', 'lg', 'O00s', 'O10s', 'R00f', 'r02', 'r12', 'g2', 'R10s', 'R00e', 'O00f', 'O10f', 'r03', 'r13', 'R10f', 're0', 'ps', 're1', 'O00e', 'O10e', 'O01s', 'O11s', 'R10e', 'R01s', 'R11s', 'ph', 't00', 't10', 'og', 'd00', 'd10', 'O01f', 'O11f', 'sg', 'S00s', 'S10s', 't01', 't11', 'd01', 'd11', 'O01e', 'O11e', 'O0c', 'O1c', 'Y0', 'S00f', 'S10f', 'R01f', 'R11f', 't02', 't12', 'd02', 'd12', 'S00e', 'S10e', 'S01s', 'S11s', 'R01e', 'R11e', 't03', 't13', 'Y1', 'S01f', 'S11f', 'd03', 'd13', 'S01e', 'S11e', 'R0c', 'R1c', 'S0c', 'S1c', 'K', 'L', 'de0', 'de1', 'X', 'te0', 'te1', 'U', 'F')


def dot(a, b):
    return jnp.dot(a, b, preferred_element_type=F32)


def kernel(a_ref, piv_ref, linv_ref, uinv_ref, out_ref,
           srcb, destr, contrib, rs_long, rs_short, top_own, old_own, pan, top_pan,
           left, tx, ux, pick, place, moved,
           sem_rs, rem_rs, sem_tz, rem_tz, sem_dz, rem_dz,
           sem_sc, rem_sc, sem_mir, rem_mir, loc_sem, sem_ds, rem_ds,
           sem_ts, rem_ts, sem_tsl, rem_tsl,
           sem_ring, rem_ring, sem_par, rem_par):
    r = lax.axis_index("prow")
    q = lax.axis_index("pcol")
    x = q // 8
    y = (q // 2) % 4
    core = q % 2
    g = core * 4 + x

    def panel_of(yy):
        return (yy % 3 + 1) * ((yy + 3) // 4)

    p = panel_of(y)
    home_y = ((q + 1) % 3 + 1) * ((q + 3) // 4)

    def dev(rr, qq):
        return (rr, qq)

    def at_q(xx, yy, cc):
        return xx * 8 + yy * 2 + cc

    def plane(off):
        return (r + off + NZ) % NZ

    def rcopy(src, dst, ssem, rsem, where):
        return pltpu.make_async_remote_copy(
            src_ref=src, dst_ref=dst, send_sem=ssem, recv_sem=rsem,
            device_id=where, device_id_type=pl.DeviceIdType.MESH)

    def got(dst, ssem, rsem, where):
        rcopy(dst, dst, ssem, rsem, where).wait_recv()

    def sent(src, ssem, rsem, where):
        rcopy(src, src, ssem, rsem, where).wait_send()

    x_up, x_dn = at_q((x + 1) % 4, y, core), at_q((x + 3) % 4, y, core)
    y_up, y_dn = at_q(x, (y + 1) % 4, core), at_q(x, (y + 3) % 4, core)
    mate = at_q(x, y, 1 - core)

    barrier = pltpu.get_barrier_semaphore()

    def greet(where):
        pl.semaphore_signal(barrier, inc=1, device_id=where, device_id_type=pl.DeviceIdType.MESH)

    for off in range(1, NZ):
        greet(dev(plane(off), q))
    for other in (x_up, x_dn, y_up, y_dn, mate):
        greet(dev(r, other))

    keeps = (q == 0) | (q == 2)
    gives = (q == 1) | (q == 3)

    @pl.when(jnp.logical_not(keeps))
    def _():
        greet(dev(r, p))

    @pl.when(gives)
    def _():
        greet(dev(r, at_q(0, home_y, 0)))

    @pl.when(q < 4)
    def _():
        for t in range(1, 8):
            greet(dev(r, at_q(t % 4, home_y, t // 4)))

    def colb(row):
        return jnp.transpose(jnp.broadcast_to(row, (128, 128)))

    pts = []
    for s in range(4):
        row = piv_ref[s:s + 1, :].astype(F32)
        pts.append(jnp.concatenate([colb(row[:, :128]), colb(row[:, 128:])], axis=0))
    sub = lax.broadcasted_iota(jnp.int32, (NB, 128), 0).astype(F32)
    lane = lax.broadcasted_iota(jnp.int32, (1, 128), 1).astype(F32)

    def swap(cur, s):
        target = sub + float(s * NB)
        delta = pts[s] - target
        move = jnp.where(target == cur, delta, 0.0) - jnp.where(pts[s] == cur, delta, 0.0)
        return cur + jnp.sum(move, axis=0, keepdims=True)

    def perm_tile(t, carry):
        start = lane + (t * 128).astype(F32)
        cur = start
        for s in (3, 2, 1, 0):
            cur = swap(cur, s)
        srcb[pl.ds(pl.multiple_of(t * 128, 128), 128), :] = colb(cur)
        cur = start
        for s in (0, 1, 2, 3):
            cur = swap(cur, s)
        destr[t] = cur
        return carry

    lax.fori_loop(0, 8, perm_tile, 0)

    @pl.when(keeps)
    def _():
        pl.semaphore_wait(barrier, 19)

    @pl.when(gives)
    def _():
        pl.semaphore_wait(barrier, 21)

    @pl.when(q >= 4)
    def _():
        pl.semaphore_wait(barrier, 13)

    groups = ((0, 1), (1, 3), (4, 4))

    def scatter_raw(t, n):
        lo, size = groups[n]
        return rcopy(a_ref.at[pl.ds(lo, size), pl.ds(32 * t, 32), pl.ds(0, NB)],
                     pan.at[pl.ds(lo, size), pl.ds(32 * t, 32), pl.ds(pl.multiple_of(NB * q, NB), NB)],
                     sem_sc.at[8 * n + t], rem_sc.at[n], dev(r, at_q(t % 4, home_y, t // 4)))

    def raw_self(n):
        lo, size = groups[n]
        return pltpu.make_async_copy(
            a_ref.at[pl.ds(lo, size), pl.ds(0, 32), pl.ds(0, NB)],
            pan.at[pl.ds(lo, size), pl.ds(0, 32), pl.ds(pl.multiple_of(NB * q, NB), NB)],
            loc_sem.at[3 + n])

    def raw_start(n):
        @pl.when(keeps)
        def _():
            raw_self(n).start()

        @pl.when(gives)
        def _():
            scatter_raw(0, n).start()

        @pl.when(q < 4)
        def _():
            for t in range(1, 8):
                scatter_raw(t, n).start()

    def raw_wait(n):
        lo, size = groups[n]

        @pl.when(keeps)
        def _():
            raw_self(n).wait()

        @pl.when(jnp.logical_not(keeps))
        def _():
            got(pan.at[pl.ds(lo, size), mine32, minec], sem_sc.at[0], rem_sc.at[n], dev(r, mate))

    def mirror():
        return rcopy(a_ref.at[0, pl.ds(128, 128), :],
                     old_own.at[r % 4, pl.ds(128, 128), :],
                     sem_mir.at[0], rem_mir.at[0], dev(7 - r, q))

    def old_self():
        return pltpu.make_async_copy(a_ref.at[0, pl.ds(0, 128), :],
                                     old_own.at[r % 4, pl.ds(0, 128), :], loc_sem.at[1])

    def contribute(h):
        def body(i, carry):
            cs = pl.ds(4 * i, 4)
            if h == 0:
                for j in range(4):
                    c = 4 * i + j
                    want = srcb[pl.ds(pl.multiple_of(c * 128, 128), 128), :]
                    for t in range(16):
                        gid = lane + ((t // 2 * NZ + r) * NB + (t % 2) * 128).astype(F32)
                        pick[c, :, 128 * t:128 * (t + 1)] = jnp.where(want == gid, 1.0, 0.0).astype(BF)
            rows = dot(pick[cs].reshape(512, 2048), a_ref[:, :, NB * h:NB * (h + 1)].reshape(2048, NB))
            contrib[cs, :, NB * h:NB * (h + 1)] = rows.astype(BF).reshape(4, 128, NB)
            return carry

        lax.fori_loop(0, 2, body, 0)

    def half(h):
        return pl.ds(NB * h, NB)

    def delta(h):
        return 1 if h == 0 else -1

    def rs_send(h, way, k):
        d = delta(h) if way == 0 else -delta(h)
        buf = rs_long if way == 0 else rs_short
        first = 4 if way == 0 else 3
        src = contrib.at[plane(first * d), :, half(h)] if k == 0 else buf.at[h, k - 1]
        idx = h * 7 + way * 4 + k
        return rcopy(src, buf.at[h, k], sem_rs.at[idx], rem_rs.at[idx], dev(plane(d), q))

    def rs_step(h, way, k):
        d = delta(h) if way == 0 else -delta(h)
        buf = rs_long if way == 0 else rs_short
        first = 4 if way == 0 else 3
        rs_send(h, way, k - 1).wait_recv()
        buf[h, k - 1] = buf[h, k - 1] + contrib[plane((first - k) * d), :, NB * h:NB * (h + 1)]
        rs_send(h, way, k).start()

    def rs_end(h):
        rs_send(h, 0, 3).wait_recv()
        rs_send(h, 1, 2).wait_recv()
        top_own[r, :, NB * h:NB * (h + 1)] = (
            contrib[r, :, NB * h:NB * (h + 1)] + rs_long[h, 3] + rs_short[h, 2])

    def top_view(j, h):
        return top_own.at[j, :, half(h)]

    def old_view(j, h):
        hi = j // 4
        a = j + hi * (7 - 2 * j)
        return old_own.at[a, pl.ds(pl.multiple_of(128 * hi, 128), 128), half(h)]

    def zag(view, ssem, rsem, h, way, k):
        d = delta(h) if way == 0 else -delta(h)
        idx = h * 7 + way * 4 + k
        v = view(plane(-k * d), h)
        return rcopy(v, v, ssem.at[idx], rsem.at[idx], dev(plane(d), q))

    def zag_got(view, ssem, rsem, h, way, k):
        d = delta(h) if way == 0 else -delta(h)
        idx = h * 7 + way * 4 + k
        got(view(plane(-(k + 1) * d), h), ssem.at[idx], rsem.at[idx], dev(plane(d), q))

    def zag_step(view, ssem, rsem, h, k):
        for way in range(2):
            if k < 4 - way:
                if k > 0:
                    zag_got(view, ssem, rsem, h, way, k - 1)
                zag(view, ssem, rsem, h, way, k).start()

    def zag_end(view, ssem, rsem, h):
        zag_got(view, ssem, rsem, h, 0, 3)
        zag_got(view, ssem, rsem, h, 1, 2)

    top_z = (top_view, sem_tz, rem_tz)
    old_z = (old_view, sem_dz, rem_dz)

    class Ring:
        def __init__(self, buf, first, n0, rows, base):
            self.buf, self.first, self.n0, self.rows, self.base = buf, first, n0, rows, base

        def reg(self, part, stage, j, piece=None):
            n0, rows = self.n0, self.rows
            lo, n = (0, n0 // 2) if part == 0 else (n0 // 2, n0 // 2)
            if piece is not None:
                n = n // 2
                lo = lo + n * piece
            k = pl.ds(self.first + lo, n)
            along_y = (part == 0) == (stage == 0)
            if stage == 0:
                col = panel_of(j) if along_y else p
                gg = g if along_y else core * 4 + j
                return self.buf.at[k, pl.ds(pl.multiple_of(rows * gg, rows), rows),
                                   pl.ds(pl.multiple_of(NB * col, NB), NB)]
            if part == 0:
                gg = core * 4 + j
                return self.buf.at[k, pl.ds(pl.multiple_of(rows * gg, rows), rows), :]
            return self.buf.at[k, pl.ds(pl.multiple_of(4 * rows * core, 4 * rows), 4 * rows),
                               pl.ds(pl.multiple_of(NB * panel_of(j), NB), NB)]

        def copy(self, part, stage, which):
            along_y = (part == 0) == (stage == 0)
            m = y if along_y else x
            up, dn = (y_up, y_dn) if along_y else (x_up, x_dn)
            idx = self.base + (part * 2 + stage) * 4 + which
            if which < 2:
                v = self.reg(part, stage, m)
            elif which == 2:
                v = self.reg(part, stage, (m + 3) % 4, 0)
            else:
                v = self.reg(part, stage, (m + 1) % 4, 1)
            return rcopy(v, v, sem_ring.at[idx], rem_ring.at[idx], dev(r, up if which % 2 == 0 else dn))

        def wait(self, part, stage, which):
            along_y = (part == 0) == (stage == 0)
            m = y if along_y else x
            idx = self.base + (part * 2 + stage) * 4 + which
            if which == 0:
                v = self.reg(part, stage, (m + 3) % 4)
            elif which == 1:
                v = self.reg(part, stage, (m + 1) % 4)
            else:
                v = self.reg(part, stage, (m + 2) % 4, which - 2)
            got(v, sem_ring.at[idx], rem_ring.at[idx], dev(r, mate))

        def par_view(self, part, piece):
            along_y = part == 1
            m = y if along_y else x
            return m, (0, 3, 1, 2)[piece]

        def par(self, part, piece):
            m, o = self.par_view(part, piece)
            v = self.reg(part, 1, (m + o) % 4)
            idx = self.base // 2 + part * 4 + piece
            return rcopy(v, v, sem_par.at[idx], rem_par.at[idx], dev(r, mate))

        def par_wait(self, part, piece):
            m, o = self.par_view(part, piece)
            v = self.reg_other(part, (m + o) % 4)
            idx = self.base // 2 + part * 4 + piece
            got(v, sem_par.at[idx], rem_par.at[idx], dev(r, mate))

        def reg_other(self, part, j):
            n0, rows = self.n0, self.rows
            oc = 1 - core
            if part == 0:
                gg = oc * 4 + j
                return self.buf.at[pl.ds(self.first, n0 // 2), pl.ds(pl.multiple_of(rows * gg, rows), rows), :]
            return self.buf.at[pl.ds(self.first + n0 // 2, n0 // 2),
                               pl.ds(pl.multiple_of(4 * rows * oc, 4 * rows), 4 * rows),
                               pl.ds(pl.multiple_of(NB * panel_of(j), NB), NB)]

        def start(self, stage, part):
            self.copy(part, stage, 0).start()
            self.copy(part, stage, 1).start()

        def forward(self, stage, part):
            self.wait(part, stage, 0)
            self.copy(part, stage, 2).start()
            self.wait(part, stage, 1)
            self.copy(part, stage, 3).start()
            if stage == 1:
                self.par(part, 1).start()
                self.par(part, 2).start()

        def finish(self, stage, part):
            self.wait(part, stage, 2)
            self.wait(part, stage, 3)
            self.par(part, 0 if stage == 0 else 3).start()

        def close(self, part):
            for piece in range(4):
                self.par_wait(part, piece)

        def drain(self):
            for part in range(2):
                for stage in range(2):
                    for which in range(4):
                        self.copy(part, stage, which).wait_send()
                for piece in range(4):
                    self.par(part, piece).wait_send()

    ring_raw = Ring(pan, 0, 8, 32, 0)
    ring_top = Ring(top_pan, 0, 8, 16, 16)
    ring_old = Ring(pan, 8, 4, 32, 32)

    mine32 = pl.ds(pl.multiple_of(32 * g, 32), 32)
    mine16 = pl.ds(pl.multiple_of(16 * g, 16), 16)
    minec = pl.ds(pl.multiple_of(NB * p, NB), NB)

    def old_slice(off):
        return rcopy(pan.at[0, mine32, minec], pan.at[8 + r % 4, mine32, minec],
                     sem_ds.at[off - 1], rem_ds.at[r % 4], dev(plane(off), q))

    def old_slice_self():
        return pltpu.make_async_copy(pan.at[0, mine32, minec], pan.at[8 + r % 4, mine32, minec],
                                     loc_sem.at[0])

    def top_piece(t):
        return rcopy(top_own.at[r, pl.ds(16 * t, 16), pl.ds(0, NB)],
                     top_pan.at[r, pl.ds(16 * t, 16), pl.ds(pl.multiple_of(NB * q, NB), NB)],
                     sem_ts.at[t], rem_ts.at[0], dev(r, at_q(t % 4, home_y, t // 4)))

    def top_piece_self():
        return pltpu.make_async_copy(
            top_own.at[r, pl.ds(0, 16), pl.ds(0, NB)],
            top_pan.at[r, pl.ds(0, 16), pl.ds(pl.multiple_of(NB * q, NB), NB)], loc_sem.at[2])

    def top_slice(off):
        v = top_pan.at[r, mine16, minec]
        return rcopy(v, v, sem_tsl.at[off - 1], rem_tsl.at[r], dev(plane(off), q))

    row_id = lax.broadcasted_iota(jnp.int32, (NB, 1), 0).astype(F32)

    def find_places(k, carry):
        mine = row_id + ((k * NZ + r) * NB).astype(F32)
        seen = None
        for t in range(8):
            hit = jnp.where(destr[t] == mine, 1.0, 0.0)
            seen = hit if seen is None else seen + hit
            place[k, :, 128 * t:128 * (t + 1)] = hit.astype(BF)
        moved[k] = jnp.broadcast_to(jnp.sum(seen, axis=1, keepdims=True), (NB, 128))
        return carry

    def displaced_own(i, carry):
        ks = pl.ds(2 * i, 2)
        rows = dot(place[ks].reshape(512, TOP), old_own[...].reshape(TOP, COLS)).reshape(2, NB, COLS)
        for j in range(2):
            k = 2 * i + j
            out_ref[k] = jnp.where(moved[k][:, 0:1] > 0.5, rows[j], a_ref[k].astype(F32)).astype(BF)
        return carry

    def displaced_panel(i, carry):
        ks = pl.ds(2 * i, 2)
        rows = dot(place[ks].reshape(512, TOP), pan[8:12].reshape(TOP, TOP))
        left[ks] = rows.astype(BF).reshape(2, NB, TOP)
        return carry

    def top_steps():
        tx[...] = top_pan[...].reshape(TOP, TOP)
        for s in range(3):
            b, e = s * NB, (s + 1) * NB
            l_top = dot(tx[e:, b:e], uinv_ref[s]).astype(BF)
            tx[e:, b:e] = l_top
            u_pan = dot(linv_ref[s], tx[b:e, e:]).astype(BF)
            tx[b:e, e:] = u_pan
            tx[e:, e:] = (tx[e:, e:].astype(F32) - dot(l_top, u_pan)).astype(BF)

    def own_steps():
        ux[...] = top_own[...].reshape(TOP, COLS)
        for s in range(4):
            b, e = s * NB, (s + 1) * NB
            u_own = dot(linv_ref[s], ux[b:e, :]).astype(BF)
            ux[b:e, :] = u_own
            if s < 3:
                ux[e:, :] = (ux[e:, :].astype(F32) - dot(tx[e:, b:e], u_own)).astype(BF)

    TWO = 2

    def below_left(i, carry):
        ks = pl.ds(TWO * i, TWO)
        m = TWO * NB
        for j in range(TWO):
            k = TWO * i + j
            took = moved[k][:, 0:1] > 0.5
            left[k] = jnp.where(took, left[k].astype(F32), pan[k].astype(F32)).astype(BF)
        for s in range(4):
            b, e = s * NB, (s + 1) * NB
            l_row = dot(left[ks, :, b:e].reshape(m, NB), uinv_ref[s]).astype(BF)
            left[ks, :, b:e] = l_row.reshape(TWO, NB, NB)
            if s < 3:
                rest = left[ks, :, e:].reshape(m, TOP - e).astype(F32)
                left[ks, :, e:] = (rest - dot(l_row, tx[b:e, e:])).astype(BF).reshape(TWO, NB, TOP - e)
        return carry

    mycol = pl.ds(pl.multiple_of(NB * jnp.minimum(q, 3), NB), NB)

    def below_rest(i, carry):
        ks = pl.ds(TWO * i, TWO)
        m = TWO * NB
        rest = out_ref[ks].reshape(m, COLS).astype(F32)
        rest = rest - dot(left[ks].reshape(m, TOP), ux[...])
        out_ref[ks] = rest.astype(BF).reshape(TWO, NB, COLS)

        @pl.when(q < 4)
        def _():
            out_ref[ks, :, 0:NB] = left[ks, :, mycol]

        return carry

    def ev_old_send():
        @pl.when(r < 4)
        def _():
            mirror().start()
            old_self().start()

    def ev_old_got():
        @pl.when(r < 4)
        def _():
            old_self().wait()

        @pl.when(r >= 4)
        def _():
            got(old_own.at[(7 - r) % 4, pl.ds(128, 128), :], sem_mir.at[0], rem_mir.at[0], dev(7 - r, q))

    def ev_piece_send():
        @pl.when(keeps)
        def _():
            top_piece_self().start()

        @pl.when(gives)
        def _():
            top_piece(0).start()

        @pl.when(q < 4)
        def _():
            for t in range(1, 8):
                top_piece(t).start()

    def ev_piece_got():
        @pl.when(keeps)
        def _():
            top_piece_self().wait()

        @pl.when(jnp.logical_not(keeps))
        def _():
            got(top_pan.at[r, mine16, minec], sem_ts.at[0], rem_ts.at[0], dev(r, mate))

        for off in range(1, NZ):
            top_slice(off).start()

    def ev_slice_got():
        for off in range(1, NZ):
            src = plane(off)
            got(top_pan.at[src, mine16, minec], sem_tsl.at[0], rem_tsl.at[src], dev(r, mate))

    def ev_oldsl_send():
        @pl.when(r < 4)
        def _():
            old_slice_self().start()
            for off in range(1, NZ):
                old_slice(off).start()

    def ev_oldsl_got():
        for a in range(4):
            @pl.when(r != a)
            def _():
                got(pan.at[8 + a, mine32, minec], sem_ds.at[0], rem_ds.at[a], dev(r, mate))

        @pl.when(r < 4)
        def _():
            old_slice_self().wait()

    def ev_rs0(h):
        rs_send(h, 0, 0).start()
        rs_send(h, 1, 0).start()

    def ev_rs(h, k):
        rs_step(h, 0, k)
        if k < 3:
            rs_step(h, 1, k)

    todo = {
        "C0": lambda: contribute(0), "C1": lambda: contribute(1),
        "os": ev_old_send, "og": ev_old_got, "ps": ev_piece_send, "ph": ev_piece_got,
        "sg": ev_slice_got, "ls": ev_oldsl_send, "lg": ev_oldsl_got,
        "P": lambda: lax.fori_loop(0, 8, find_places, 0),
        "X": lambda: lax.fori_loop(0, 4, displaced_own, 0),
        "Y0": lambda: lax.fori_loop(0, 2, displaced_panel, 0),
        "Y1": lambda: lax.fori_loop(2, 4, displaced_panel, 0),
        "K": top_steps, "U": own_steps,
        "L": lambda: lax.fori_loop(0, 8 // TWO, below_left, 0),
        "F": lambda: lax.fori_loop(0, 8 // TWO, below_rest, 0),
    }
    for n in range(3):
        todo["w%d" % n] = lambda n=n: raw_start(n)
        todo["g%d" % n] = lambda n=n: raw_wait(n)
    for h in range(2):
        todo["r%d0" % h] = lambda h=h: ev_rs0(h)
        for k in range(1, 4):
            todo["r%d%d" % (h, k)] = lambda h=h, k=k: ev_rs(h, k)
        todo["re%d" % h] = lambda h=h: rs_end(h)
        for k in range(4):
            todo["t%d%d" % (h, k)] = lambda h=h, k=k: zag_step(*top_z, h, k)
            todo["d%d%d" % (h, k)] = lambda h=h, k=k: zag_step(*old_z, h, k)
        todo["te%d" % h] = lambda h=h: zag_end(*top_z, h)
        todo["de%d" % h] = lambda h=h: zag_end(*old_z, h)
    for name, ring in (("R", ring_raw), ("S", ring_top), ("O", ring_old)):
        for part in range(2):
            for stage in range(2):
                for verb, f in (("s", ring.start), ("f", ring.forward), ("e", ring.finish)):
                    todo["%s%d%d%s" % (name, part, stage, verb)] = (
                        lambda f=f, stage=stage, part=part: f(stage, part))
            todo["%s%dc" % (name, part)] = lambda ring=ring, part=part: ring.close(part)
    for name in ORDER:
        todo[name]()

    toprow = pl.ds(pl.multiple_of(NB * jnp.minimum(r, 3), NB), NB)

    @pl.when(r < 4)
    def _():
        out_ref[0] = ux[toprow, :]

        @pl.when(q < 4)
        def _():
            out_ref[0, :, 0:NB] = tx[toprow, mycol]

    @pl.when(gives)
    def _():
        for n in range(3):
            scatter_raw(0, n).wait_send()
        top_piece(0).wait_send()

    @pl.when(q < 4)
    def _():
        for t in range(1, 8):
            for n in range(3):
                scatter_raw(t, n).wait_send()
            top_piece(t).wait_send()

    @pl.when(r < 4)
    def _():
        mirror().wait_send()
        for off in range(1, NZ):
            old_slice(off).wait_send()

    for off in range(1, NZ):
        top_slice(off).wait_send()
    for h in range(2):
        for way in range(2):
            for k in range(4 - way):
                rs_send(h, way, k).wait_send()
                zag(*top_z, h, way, k).wait_send()
                zag(*old_z, h, way, k).wait_send()
    ring_raw.drain()
    ring_top.drain()
    ring_old.drain()


def local(matrix, pivots, lower_inverse, upper_inverse):
    rows = matrix.reshape(256, 8, 2, NB).transpose(0, 2, 1, 3)
    a = lax.optimization_barrier(rows).transpose(0, 2, 1, 3).reshape(8, NB, COLS)
    vm = pl.BlockSpec(memory_space=pltpu.VMEM)
    dma = pltpu.SemaphoreType.DMA
    out = pl.pallas_call(
        kernel,
        out_shape=jax.ShapeDtypeStruct((8, NB, COLS), BF),
        in_specs=[vm] * 4,
        out_specs=vm,
        scratch_shapes=[
            pltpu.VMEM((TOP, 128), F32),
            pltpu.VMEM((8, 1, 128), F32),
            pltpu.VMEM((8, 128, COLS), BF),
            pltpu.VMEM((2, 4, 128, NB), BF),
            pltpu.VMEM((2, 3, 128, NB), BF),
            pltpu.VMEM((8, 128, COLS), BF),
            pltpu.VMEM((4, NB, COLS), BF),
            pltpu.VMEM((12, NB, TOP), BF),
            pltpu.VMEM((8, 128, TOP), BF),
            pltpu.VMEM((8, NB, TOP), BF),
            pltpu.VMEM((TOP, TOP), BF),
            pltpu.VMEM((TOP, COLS), BF),
            pltpu.VMEM((8, 128, 2048), BF),
            pltpu.VMEM((8, NB, TOP), BF),
            pltpu.VMEM((8, NB, 128), F32),
            dma((14,)), dma((14,)), dma((14,)), dma((14,)), dma((14,)), dma((14,)),
            dma((24,)), dma((3,)), dma((1,)), dma((1,)), dma((6,)), dma((7,)), dma((4,)),
            dma((8,)), dma((1,)), dma((7,)), dma((8,)),
            dma((48,)), dma((48,)), dma((24,)), dma((24,)),
        ],
        compiler_params=pltpu.CompilerParams(
            collective_id=0, has_side_effects=True, vmem_limit_bytes=46 * 1024 * 1024),
    )(a, pivots, lower_inverse, upper_inverse)
    return out.reshape(matrix.shape)


def solution(mesh):
    placed = (P(None, "prow", None, "pcol"), P(), P(), P())
    return jax.shard_map(
        local, mesh=mesh, in_specs=placed, out_specs=P(None, "prow", None, "pcol"), check_vma=False
    )
```

```python
import jax
import jax.numpy as jnp
from jax import lax
from jax.experimental import pallas as pl
from jax.experimental.pallas import tpu as pltpu
from jax.sharding import PartitionSpec as P

BF = jnp.bfloat16
F32 = jnp.float32
NB = 256
NZ = 8
TOP = 1024
COLS = 512


ORDER = ('w0', 'w1', 'w2', 'os', 'C0', 'r00', 'C1', 'r10', 'g0', 'ls', 'r01', 'g1', 'R00s', 'P', 'r11', 'lg', 'O00s', 'O10s', 'R00f', 'r02', 'r12', 'g2', 'R10s', 'R00e', 'O00f', 'O10f', 'r03', 'r13', 'og', 'd00', 'd10', 'R10f', 're0', 'ps', 're1', 'O00e', 'O10e', 'O01s', 'O11s', 'R10e', 'R01s', 'R11s', 'ph', 'd01', 'd11', 't00', 't10', 'O01f', 'O11f', 'sg', 'S00s', 'S10s', 'd02', 'd12', 't01', 't11', 'O01e', 'O11e', 'O0c', 'O1c', 'd03', 'd13', 'Y0', 'S00f', 'S10f', 'R01f', 'R11f', 't02', 't12', 'Y1', 'S00e', 'S10e', 'S01s', 'S11s', 'de0', 'de1', 'X', 'R01e', 'R11e', 't03', 't13', 'S01f', 'S11f', 'S01e', 'S11e', 'R0c', 'R1c', 'S0c', 'S1c', 'K', 'L', 'te0', 'te1', 'U', 'F')


def dot(a, b):
    return jnp.dot(a, b, preferred_element_type=F32)


def kernel(a_ref, piv_ref, linv_ref, uinv_ref, out_ref,
           srcb, destr, contrib, rs_long, rs_short, top_own, old_own, pan, top_pan,
           left, tx, ux, pick, place, moved,
           sem_rs, rem_rs, sem_tz, rem_tz, sem_dz, rem_dz,
           sem_sc, rem_sc, sem_mir, rem_mir, loc_sem, sem_ds, rem_ds,
           sem_ts, rem_ts, sem_tsl, rem_tsl,
           sem_ring, rem_ring, sem_par, rem_par):
    r = lax.axis_index("prow")
    q = lax.axis_index("pcol")
    x = q // 8
    y = (q // 2) % 4
    core = q % 2
    g = core * 4 + x

    def panel_of(yy):
        return (yy % 3 + 1) * ((yy + 3) // 4)

    p = panel_of(y)
    home_y = ((q + 1) % 3 + 1) * ((q + 3) // 4)

    def dev(rr, qq):
        return (rr, qq)

    def at_q(xx, yy, cc):
        return xx * 8 + yy * 2 + cc

    def plane(off):
        return (r + off + NZ) % NZ

    def rcopy(src, dst, ssem, rsem, where):
        return pltpu.make_async_remote_copy(
            src_ref=src, dst_ref=dst, send_sem=ssem, recv_sem=rsem,
            device_id=where, device_id_type=pl.DeviceIdType.MESH)

    def got(dst, ssem, rsem, where):
        rcopy(dst, dst, ssem, rsem, where).wait_recv()

    def sent(src, ssem, rsem, where):
        rcopy(src, src, ssem, rsem, where).wait_send()

    x_up, x_dn = at_q((x + 1) % 4, y, core), at_q((x + 3) % 4, y, core)
    y_up, y_dn = at_q(x, (y + 1) % 4, core), at_q(x, (y + 3) % 4, core)
    mate = at_q(x, y, 1 - core)

    barrier = pltpu.get_barrier_semaphore()

    def greet(where):
        pl.semaphore_signal(barrier, inc=1, device_id=where, device_id_type=pl.DeviceIdType.MESH)

    for off in range(1, NZ):
        greet(dev(plane(off), q))
    for other in (x_up, x_dn, y_up, y_dn, mate):
        greet(dev(r, other))

    keeps = (q == 0) | (q == 2)
    gives = (q == 1) | (q == 3)

    @pl.when(jnp.logical_not(keeps))
    def _():
        greet(dev(r, p))

    @pl.when(gives)
    def _():
        greet(dev(r, at_q(0, home_y, 0)))

    @pl.when(q < 4)
    def _():
        for t in range(1, 8):
            greet(dev(r, at_q(t % 4, home_y, t // 4)))

    def colb(row):
        return jnp.transpose(jnp.broadcast_to(row, (128, 128)))

    pts = []
    for s in range(4):
        row = piv_ref[s:s + 1, :].astype(F32)
        pts.append(jnp.concatenate([colb(row[:, :128]), colb(row[:, 128:])], axis=0))
    sub = lax.broadcasted_iota(jnp.int32, (NB, 128), 0).astype(F32)
    lane = lax.broadcasted_iota(jnp.int32, (1, 128), 1).astype(F32)

    def swap(cur, s):
        target = sub + float(s * NB)
        delta = pts[s] - target
        move = jnp.where(target == cur, delta, 0.0) - jnp.where(pts[s] == cur, delta, 0.0)
        return cur + jnp.sum(move, axis=0, keepdims=True)

    def perm_tile(t, carry):
        start = lane + (t * 128).astype(F32)
        cur = start
        for s in (3, 2, 1, 0):
            cur = swap(cur, s)
        srcb[pl.ds(pl.multiple_of(t * 128, 128), 128), :] = colb(cur)
        cur = start
        for s in (0, 1, 2, 3):
            cur = swap(cur, s)
        destr[t] = cur
        return carry

    lax.fori_loop(0, 8, perm_tile, 0)

    @pl.when(keeps)
    def _():
        pl.semaphore_wait(barrier, 19)

    @pl.when(gives)
    def _():
        pl.semaphore_wait(barrier, 21)

    @pl.when(q >= 4)
    def _():
        pl.semaphore_wait(barrier, 13)

    groups = ((0, 1), (1, 3), (4, 4))

    def scatter_raw(t, n):
        lo, size = groups[n]
        return rcopy(a_ref.at[pl.ds(lo, size), pl.ds(32 * t, 32), pl.ds(0, NB)],
                     pan.at[pl.ds(lo, size), pl.ds(32 * t, 32), pl.ds(pl.multiple_of(NB * q, NB), NB)],
                     sem_sc.at[8 * n + t], rem_sc.at[n], dev(r, at_q(t % 4, home_y, t // 4)))

    def raw_self(n):
        lo, size = groups[n]
        return pltpu.make_async_copy(
            a_ref.at[pl.ds(lo, size), pl.ds(0, 32), pl.ds(0, NB)],
            pan.at[pl.ds(lo, size), pl.ds(0, 32), pl.ds(pl.multiple_of(NB * q, NB), NB)],
            loc_sem.at[3 + n])

    def raw_start(n):
        @pl.when(keeps)
        def _():
            raw_self(n).start()

        @pl.when(gives)
        def _():
            scatter_raw(0, n).start()

        @pl.when(q < 4)
        def _():
            for t in range(1, 8):
                scatter_raw(t, n).start()

    def raw_wait(n):
        lo, size = groups[n]

        @pl.when(keeps)
        def _():
            raw_self(n).wait()

        @pl.when(jnp.logical_not(keeps))
        def _():
            got(pan.at[pl.ds(lo, size), mine32, minec], sem_sc.at[0], rem_sc.at[n], dev(r, mate))

    def mirror():
        return rcopy(a_ref.at[0, pl.ds(128, 128), :],
                     old_own.at[r % 4, pl.ds(128, 128), :],
                     sem_mir.at[0], rem_mir.at[0], dev(7 - r, q))

    def old_self():
        return pltpu.make_async_copy(a_ref.at[0, pl.ds(0, 128), :],
                                     old_own.at[r % 4, pl.ds(0, 128), :], loc_sem.at[1])

    def contribute(h):
        def body(i, carry):
            cs = pl.ds(4 * i, 4)
            if h == 0:
                for j in range(4):
                    c = 4 * i + j
                    want = srcb[pl.ds(pl.multiple_of(c * 128, 128), 128), :]
                    for t in range(16):
                        gid = lane + ((t // 2 * NZ + r) * NB + (t % 2) * 128).astype(F32)
                        pick[c, :, 128 * t:128 * (t + 1)] = jnp.where(want == gid, 1.0, 0.0).astype(BF)
            rows = dot(pick[cs].reshape(512, 2048), a_ref[:, :, NB * h:NB * (h + 1)].reshape(2048, NB))
            contrib[cs, :, NB * h:NB * (h + 1)] = rows.astype(BF).reshape(4, 128, NB)
            return carry

        lax.fori_loop(0, 2, body, 0)

    def half(h):
        return pl.ds(NB * h, NB)

    def delta(h):
        return 1 if h == 0 else -1

    def rs_send(h, way, k):
        d = delta(h) if way == 0 else -delta(h)
        buf = rs_long if way == 0 else rs_short
        first = 4 if way == 0 else 3
        src = contrib.at[plane(first * d), :, half(h)] if k == 0 else buf.at[h, k - 1]
        idx = h * 7 + way * 4 + k
        return rcopy(src, buf.at[h, k], sem_rs.at[idx], rem_rs.at[idx], dev(plane(d), q))

    def rs_step(h, way, k):
        d = delta(h) if way == 0 else -delta(h)
        buf = rs_long if way == 0 else rs_short
        first = 4 if way == 0 else 3
        rs_send(h, way, k - 1).wait_recv()
        buf[h, k - 1] = buf[h, k - 1] + contrib[plane((first - k) * d), :, NB * h:NB * (h + 1)]
        rs_send(h, way, k).start()

    def rs_end(h):
        rs_send(h, 0, 3).wait_recv()
        rs_send(h, 1, 2).wait_recv()
        top_own[r, :, NB * h:NB * (h + 1)] = (
            contrib[r, :, NB * h:NB * (h + 1)] + rs_long[h, 3] + rs_short[h, 2])

    def top_view(j, h):
        return top_own.at[j, :, half(h)]

    def old_view(j, h):
        hi = j // 4
        a = j + hi * (7 - 2 * j)
        return old_own.at[a, pl.ds(pl.multiple_of(128 * hi, 128), 128), half(h)]

    def zag(view, ssem, rsem, h, way, k):
        d = delta(h) if way == 0 else -delta(h)
        idx = h * 7 + way * 4 + k
        v = view(plane(-k * d), h)
        return rcopy(v, v, ssem.at[idx], rsem.at[idx], dev(plane(d), q))

    def zag_got(view, ssem, rsem, h, way, k):
        d = delta(h) if way == 0 else -delta(h)
        idx = h * 7 + way * 4 + k
        got(view(plane(-(k + 1) * d), h), ssem.at[idx], rsem.at[idx], dev(plane(d), q))

    def zag_step(view, ssem, rsem, h, k):
        for way in range(2):
            if k < 4 - way:
                if k > 0:
                    zag_got(view, ssem, rsem, h, way, k - 1)
                zag(view, ssem, rsem, h, way, k).start()

    def zag_end(view, ssem, rsem, h):
        zag_got(view, ssem, rsem, h, 0, 3)
        zag_got(view, ssem, rsem, h, 1, 2)

    top_z = (top_view, sem_tz, rem_tz)
    old_z = (old_view, sem_dz, rem_dz)

    class Ring:
        def __init__(self, buf, first, n0, rows, base):
            self.buf, self.first, self.n0, self.rows, self.base = buf, first, n0, rows, base

        def reg(self, part, stage, j, piece=None):
            n0, rows = self.n0, self.rows
            lo, n = (0, n0 // 2) if part == 0 else (n0 // 2, n0 // 2)
            if piece is not None:
                n = n // 2
                lo = lo + n * piece
            k = pl.ds(self.first + lo, n)
            along_y = (part == 0) == (stage == 0)
            if stage == 0:
                col = panel_of(j) if along_y else p
                gg = g if along_y else core * 4 + j
                return self.buf.at[k, pl.ds(pl.multiple_of(rows * gg, rows), rows),
                                   pl.ds(pl.multiple_of(NB * col, NB), NB)]
            if part == 0:
                gg = core * 4 + j
                return self.buf.at[k, pl.ds(pl.multiple_of(rows * gg, rows), rows), :]
            return self.buf.at[k, pl.ds(pl.multiple_of(4 * rows * core, 4 * rows), 4 * rows),
                               pl.ds(pl.multiple_of(NB * panel_of(j), NB), NB)]

        def copy(self, part, stage, which):
            along_y = (part == 0) == (stage == 0)
            m = y if along_y else x
            up, dn = (y_up, y_dn) if along_y else (x_up, x_dn)
            idx = self.base + (part * 2 + stage) * 4 + which
            if which < 2:
                v = self.reg(part, stage, m)
            elif which == 2:
                v = self.reg(part, stage, (m + 3) % 4, 0)
            else:
                v = self.reg(part, stage, (m + 1) % 4, 1)
            return rcopy(v, v, sem_ring.at[idx], rem_ring.at[idx], dev(r, up if which % 2 == 0 else dn))

        def wait(self, part, stage, which):
            along_y = (part == 0) == (stage == 0)
            m = y if along_y else x
            idx = self.base + (part * 2 + stage) * 4 + which
            if which == 0:
                v = self.reg(part, stage, (m + 3) % 4)
            elif which == 1:
                v = self.reg(part, stage, (m + 1) % 4)
            else:
                v = self.reg(part, stage, (m + 2) % 4, which - 2)
            got(v, sem_ring.at[idx], rem_ring.at[idx], dev(r, mate))

        def par_view(self, part, piece):
            along_y = part == 1
            m = y if along_y else x
            return m, (0, 3, 1, 2)[piece]

        def par(self, part, piece):
            m, o = self.par_view(part, piece)
            v = self.reg(part, 1, (m + o) % 4)
            idx = self.base // 2 + part * 4 + piece
            return rcopy(v, v, sem_par.at[idx], rem_par.at[idx], dev(r, mate))

        def par_wait(self, part, piece):
            m, o = self.par_view(part, piece)
            v = self.reg_other(part, (m + o) % 4)
            idx = self.base // 2 + part * 4 + piece
            got(v, sem_par.at[idx], rem_par.at[idx], dev(r, mate))

        def reg_other(self, part, j):
            n0, rows = self.n0, self.rows
            oc = 1 - core
            if part == 0:
                gg = oc * 4 + j
                return self.buf.at[pl.ds(self.first, n0 // 2), pl.ds(pl.multiple_of(rows * gg, rows), rows), :]
            return self.buf.at[pl.ds(self.first + n0 // 2, n0 // 2),
                               pl.ds(pl.multiple_of(4 * rows * oc, 4 * rows), 4 * rows),
                               pl.ds(pl.multiple_of(NB * panel_of(j), NB), NB)]

        def start(self, stage, part):
            self.copy(part, stage, 0).start()
            self.copy(part, stage, 1).start()

        def forward(self, stage, part):
            self.wait(part, stage, 0)
            self.copy(part, stage, 2).start()
            self.wait(part, stage, 1)
            self.copy(part, stage, 3).start()
            if stage == 1:
                self.par(part, 1).start()
                self.par(part, 2).start()

        def finish(self, stage, part):
            self.wait(part, stage, 2)
            self.wait(part, stage, 3)
            self.par(part, 0 if stage == 0 else 3).start()

        def close(self, part):
            for piece in range(4):
                self.par_wait(part, piece)

        def drain(self):
            for part in range(2):
                for stage in range(2):
                    for which in range(4):
                        self.copy(part, stage, which).wait_send()
                for piece in range(4):
                    self.par(part, piece).wait_send()

    ring_raw = Ring(pan, 0, 8, 32, 0)
    ring_top = Ring(top_pan, 0, 8, 16, 16)
    ring_old = Ring(pan, 8, 4, 32, 32)

    mine32 = pl.ds(pl.multiple_of(32 * g, 32), 32)
    mine16 = pl.ds(pl.multiple_of(16 * g, 16), 16)
    minec = pl.ds(pl.multiple_of(NB * p, NB), NB)

    def old_slice(off):
        return rcopy(pan.at[0, mine32, minec], pan.at[8 + r % 4, mine32, minec],
                     sem_ds.at[off - 1], rem_ds.at[r % 4], dev(plane(off), q))

    def old_slice_self():
        return pltpu.make_async_copy(pan.at[0, mine32, minec], pan.at[8 + r % 4, mine32, minec],
                                     loc_sem.at[0])

    def top_piece(t):
        return rcopy(top_own.at[r, pl.ds(16 * t, 16), pl.ds(0, NB)],
                     top_pan.at[r, pl.ds(16 * t, 16), pl.ds(pl.multiple_of(NB * q, NB), NB)],
                     sem_ts.at[t], rem_ts.at[0], dev(r, at_q(t % 4, home_y, t // 4)))

    def top_piece_self():
        return pltpu.make_async_copy(
            top_own.at[r, pl.ds(0, 16), pl.ds(0, NB)],
            top_pan.at[r, pl.ds(0, 16), pl.ds(pl.multiple_of(NB * q, NB), NB)], loc_sem.at[2])

    def top_slice(off):
        v = top_pan.at[r, mine16, minec]
        return rcopy(v, v, sem_tsl.at[off - 1], rem_tsl.at[r], dev(plane(off), q))

    row_id = lax.broadcasted_iota(jnp.int32, (NB, 1), 0).astype(F32)

    def find_places(k, carry):
        mine = row_id + ((k * NZ + r) * NB).astype(F32)
        seen = None
        for t in range(8):
            hit = jnp.where(destr[t] == mine, 1.0, 0.0)
            seen = hit if seen is None else seen + hit
            place[k, :, 128 * t:128 * (t + 1)] = hit.astype(BF)
        moved[k] = jnp.broadcast_to(jnp.sum(seen, axis=1, keepdims=True), (NB, 128))
        return carry

    def displaced_own(i, carry):
        ks = pl.ds(2 * i, 2)
        rows = dot(place[ks].reshape(512, TOP), old_own[...].reshape(TOP, COLS)).reshape(2, NB, COLS)
        for j in range(2):
            k = 2 * i + j
            out_ref[k] = jnp.where(moved[k][:, 0:1] > 0.5, rows[j], a_ref[k].astype(F32)).astype(BF)
        return carry

    def displaced_panel(i, carry):
        ks = pl.ds(2 * i, 2)
        rows = dot(place[ks].reshape(512, TOP), pan[8:12].reshape(TOP, TOP))
        left[ks] = rows.astype(BF).reshape(2, NB, TOP)
        return carry

    def top_steps():
        tx[...] = top_pan[...].reshape(TOP, TOP)
        for s in range(3):
            b, e = s * NB, (s + 1) * NB
            l_top = dot(tx[e:, b:e], uinv_ref[s]).astype(BF)
            tx[e:, b:e] = l_top
            u_pan = dot(linv_ref[s], tx[b:e, e:]).astype(BF)
            tx[b:e, e:] = u_pan
            tx[e:, e:] = (tx[e:, e:].astype(F32) - dot(l_top, u_pan)).astype(BF)

    def own_steps():
        ux[...] = top_own[...].reshape(TOP, COLS)
        for s in range(4):
            b, e = s * NB, (s + 1) * NB
            u_own = dot(linv_ref[s], ux[b:e, :]).astype(BF)
            ux[b:e, :] = u_own
            if s < 3:
                ux[e:, :] = (ux[e:, :].astype(F32) - dot(tx[e:, b:e], u_own)).astype(BF)

    TWO = 2

    def below_left(i, carry):
        ks = pl.ds(TWO * i, TWO)
        m = TWO * NB
        for j in range(TWO):
            k = TWO * i + j
            took = moved[k][:, 0:1] > 0.5
            left[k] = jnp.where(took, left[k].astype(F32), pan[k].astype(F32)).astype(BF)
        for s in range(4):
            b, e = s * NB, (s + 1) * NB
            l_row = dot(left[ks, :, b:e].reshape(m, NB), uinv_ref[s]).astype(BF)
            left[ks, :, b:e] = l_row.reshape(TWO, NB, NB)
            if s < 3:
                rest = left[ks, :, e:].reshape(m, TOP - e).astype(F32)
                left[ks, :, e:] = (rest - dot(l_row, tx[b:e, e:])).astype(BF).reshape(TWO, NB, TOP - e)
        return carry

    mycol = pl.ds(pl.multiple_of(NB * jnp.minimum(q, 3), NB), NB)

    def below_rest(i, carry):
        ks = pl.ds(TWO * i, TWO)
        m = TWO * NB
        rest = out_ref[ks].reshape(m, COLS).astype(F32)
        rest = rest - dot(left[ks].reshape(m, TOP), ux[...])
        out_ref[ks] = rest.astype(BF).reshape(TWO, NB, COLS)

        @pl.when(q < 4)
        def _():
            out_ref[ks, :, 0:NB] = left[ks, :, mycol]

        return carry

    def ev_old_send():
        @pl.when(r < 4)
        def _():
            mirror().start()
            old_self().start()

    def ev_old_got():
        @pl.when(r < 4)
        def _():
            old_self().wait()

        @pl.when(r >= 4)
        def _():
            got(old_own.at[(7 - r) % 4, pl.ds(128, 128), :], sem_mir.at[0], rem_mir.at[0], dev(7 - r, q))

    def ev_piece_send():
        @pl.when(keeps)
        def _():
            top_piece_self().start()

        @pl.when(gives)
        def _():
            top_piece(0).start()

        @pl.when(q < 4)
        def _():
            for t in range(1, 8):
                top_piece(t).start()

    def ev_piece_got():
        @pl.when(keeps)
        def _():
            top_piece_self().wait()

        @pl.when(jnp.logical_not(keeps))
        def _():
            got(top_pan.at[r, mine16, minec], sem_ts.at[0], rem_ts.at[0], dev(r, mate))

        for off in range(1, NZ):
            top_slice(off).start()

    def ev_slice_got():
        for off in range(1, NZ):
            src = plane(off)
            got(top_pan.at[src, mine16, minec], sem_tsl.at[0], rem_tsl.at[src], dev(r, mate))

    def ev_oldsl_send():
        @pl.when(r < 4)
        def _():
            old_slice_self().start()
            for off in range(1, NZ):
                old_slice(off).start()

    def ev_oldsl_got():
        for a in range(4):
            @pl.when(r != a)
            def _():
                got(pan.at[8 + a, mine32, minec], sem_ds.at[0], rem_ds.at[a], dev(r, mate))

        @pl.when(r < 4)
        def _():
            old_slice_self().wait()

    def ev_rs0(h):
        rs_send(h, 0, 0).start()
        rs_send(h, 1, 0).start()

    def ev_rs(h, k):
        rs_step(h, 0, k)
        if k < 3:
            rs_step(h, 1, k)

    todo = {
        "C0": lambda: contribute(0), "C1": lambda: contribute(1),
        "os": ev_old_send, "og": ev_old_got, "ps": ev_piece_send, "ph": ev_piece_got,
        "sg": ev_slice_got, "ls": ev_oldsl_send, "lg": ev_oldsl_got,
        "P": lambda: lax.fori_loop(0, 8, find_places, 0),
        "X": lambda: lax.fori_loop(0, 4, displaced_own, 0),
        "Y0": lambda: lax.fori_loop(0, 2, displaced_panel, 0),
        "Y1": lambda: lax.fori_loop(2, 4, displaced_panel, 0),
        "K": top_steps, "U": own_steps,
        "L": lambda: lax.fori_loop(0, 8 // TWO, below_left, 0),
        "F": lambda: lax.fori_loop(0, 8 // TWO, below_rest, 0),
    }
    for n in range(3):
        todo["w%d" % n] = lambda n=n: raw_start(n)
        todo["g%d" % n] = lambda n=n: raw_wait(n)
    for h in range(2):
        todo["r%d0" % h] = lambda h=h: ev_rs0(h)
        for k in range(1, 4):
            todo["r%d%d" % (h, k)] = lambda h=h, k=k: ev_rs(h, k)
        todo["re%d" % h] = lambda h=h: rs_end(h)
        for k in range(4):
            todo["t%d%d" % (h, k)] = lambda h=h, k=k: zag_step(*top_z, h, k)
            todo["d%d%d" % (h, k)] = lambda h=h, k=k: zag_step(*old_z, h, k)
        todo["te%d" % h] = lambda h=h: zag_end(*top_z, h)
        todo["de%d" % h] = lambda h=h: zag_end(*old_z, h)
    for name, ring in (("R", ring_raw), ("S", ring_top), ("O", ring_old)):
        for part in range(2):
            for stage in range(2):
                for verb, f in (("s", ring.start), ("f", ring.forward), ("e", ring.finish)):
                    todo["%s%d%d%s" % (name, part, stage, verb)] = (
                        lambda f=f, stage=stage, part=part: f(stage, part))
            todo["%s%dc" % (name, part)] = lambda ring=ring, part=part: ring.close(part)
    for name in ORDER:
        todo[name]()

    toprow = pl.ds(pl.multiple_of(NB * jnp.minimum(r, 3), NB), NB)

    @pl.when(r < 4)
    def _():
        out_ref[0] = ux[toprow, :]

        @pl.when(q < 4)
        def _():
            out_ref[0, :, 0:NB] = tx[toprow, mycol]

    @pl.when(gives)
    def _():
        for n in range(3):
            scatter_raw(0, n).wait_send()
        top_piece(0).wait_send()

    @pl.when(q < 4)
    def _():
        for t in range(1, 8):
            for n in range(3):
                scatter_raw(t, n).wait_send()
            top_piece(t).wait_send()

    @pl.when(r < 4)
    def _():
        mirror().wait_send()
        for off in range(1, NZ):
            old_slice(off).wait_send()

    for off in range(1, NZ):
        top_slice(off).wait_send()
    for h in range(2):
        for way in range(2):
            for k in range(4 - way):
                rs_send(h, way, k).wait_send()
                zag(*top_z, h, way, k).wait_send()
                zag(*old_z, h, way, k).wait_send()
    ring_raw.drain()
    ring_top.drain()
    ring_old.drain()


def local(matrix, pivots, lower_inverse, upper_inverse):
    rows = matrix.reshape(256, 8, 2, NB).transpose(0, 2, 1, 3)
    a = lax.optimization_barrier(rows).transpose(0, 2, 1, 3).reshape(8, NB, COLS)
    vm = pl.BlockSpec(memory_space=pltpu.VMEM)
    dma = pltpu.SemaphoreType.DMA
    out = pl.pallas_call(
        kernel,
        out_shape=jax.ShapeDtypeStruct((8, NB, COLS), BF),
        in_specs=[vm] * 4,
        out_specs=vm,
        scratch_shapes=[
            pltpu.VMEM((TOP, 128), F32),
            pltpu.VMEM((8, 1, 128), F32),
            pltpu.VMEM((8, 128, COLS), BF),
            pltpu.VMEM((2, 4, 128, NB), BF),
            pltpu.VMEM((2, 3, 128, NB), BF),
            pltpu.VMEM((8, 128, COLS), BF),
            pltpu.VMEM((4, NB, COLS), BF),
            pltpu.VMEM((12, NB, TOP), BF),
            pltpu.VMEM((8, 128, TOP), BF),
            pltpu.VMEM((8, NB, TOP), BF),
            pltpu.VMEM((TOP, TOP), BF),
            pltpu.VMEM((TOP, COLS), BF),
            pltpu.VMEM((8, 128, 2048), BF),
            pltpu.VMEM((8, NB, TOP), BF),
            pltpu.VMEM((8, NB, 128), F32),
            dma((14,)), dma((14,)), dma((14,)), dma((14,)), dma((14,)), dma((14,)),
            dma((24,)), dma((3,)), dma((1,)), dma((1,)), dma((6,)), dma((7,)), dma((4,)),
            dma((8,)), dma((1,)), dma((7,)), dma((8,)),
            dma((48,)), dma((48,)), dma((24,)), dma((24,)),
        ],
        compiler_params=pltpu.CompilerParams(
            collective_id=0, has_side_effects=True, vmem_limit_bytes=46 * 1024 * 1024),
    )(a, pivots, lower_inverse, upper_inverse)
    return out.reshape(matrix.shape)


def solution(mesh):
    placed = (P(None, "prow", None, "pcol"), P(), P(), P())
    return jax.shard_map(
        local, mesh=mesh, in_specs=placed, out_specs=P(None, "prow", None, "pcol"), check_vma=False
    )
```

```python
import jax
import jax.numpy as jnp
from jax import lax
from jax.experimental import pallas as pl
from jax.experimental.pallas import tpu as pltpu
from jax.sharding import PartitionSpec as P

BF = jnp.bfloat16
F32 = jnp.float32
NB = 256
NZ = 8
TOP = 1024
COLS = 512


ORDER = ('w0', 'w1', 'w2', 'os', 'C0', 'r00', 'C1', 'r10', 'g0', 'ls', 'r01', 'g1', 'R00s', 'P', 'r11', 'lg', 'O00s', 'O10s', 'R00f', 'r02', 'r12', 'g2', 'R10s', 'R00e', 'O00f', 'O10f', 'r03', 'r13', 'og', 'd00', 'd10', 'R10f', 're0', 'ps', 're1', 'O00e', 'O10e', 'O01s', 'O11s', 'R10e', 'R01s', 'R11s', 'ph', 'd01', 'd11', 't00', 't10', 'O01f', 'O11f', 'sg', 'S00s', 'S10s', 'd02', 'd12', 't01', 't11', 'O01e', 'O11e', 'O0c', 'O1c', 'S00f', 'S10f', 'd03', 'd13', 'Y0', 'R01f', 'R11f', 't02', 't12', 'S00e', 'S10e', 'S01s', 'S11s', 'Y1', 'de0', 'de1', 't03', 't13', 'S01f', 'S11f', 'X', 'R01e', 'R11e', 'S01e', 'S11e', 'R0c', 'R1c', 'S0c', 'S1c', 'K', 'L', 'te0', 'te1', 'U', 'F')


def dot(a, b):
    return jnp.dot(a, b, preferred_element_type=F32)


def kernel(a_ref, piv_ref, linv_ref, uinv_ref, out_ref,
           srcb, destr, contrib, rs_long, rs_short, top_own, old_own, pan, top_pan,
           left, tx, ux, pick, place, moved,
           sem_rs, rem_rs, sem_tz, rem_tz, sem_dz, rem_dz,
           sem_sc, rem_sc, sem_mir, rem_mir, loc_sem, sem_ds, rem_ds,
           sem_ts, rem_ts, sem_tsl, rem_tsl,
           sem_ring, rem_ring, sem_par, rem_par):
    r = lax.axis_index("prow")
    q = lax.axis_index("pcol")
    x = q // 8
    y = (q // 2) % 4
    core = q % 2
    g = core * 4 + x

    def panel_of(yy):
        return (yy % 3 + 1) * ((yy + 3) // 4)

    p = panel_of(y)
    home_y = ((q + 1) % 3 + 1) * ((q + 3) // 4)

    def dev(rr, qq):
        return (rr, qq)

    def at_q(xx, yy, cc):
        return xx * 8 + yy * 2 + cc

    def plane(off):
        return (r + off + NZ) % NZ

    def rcopy(src, dst, ssem, rsem, where):
        return pltpu.make_async_remote_copy(
            src_ref=src, dst_ref=dst, send_sem=ssem, recv_sem=rsem,
            device_id=where, device_id_type=pl.DeviceIdType.MESH)

    def got(dst, ssem, rsem, where):
        rcopy(dst, dst, ssem, rsem, where).wait_recv()

    def sent(src, ssem, rsem, where):
        rcopy(src, src, ssem, rsem, where).wait_send()

    x_up, x_dn = at_q((x + 1) % 4, y, core), at_q((x + 3) % 4, y, core)
    y_up, y_dn = at_q(x, (y + 1) % 4, core), at_q(x, (y + 3) % 4, core)
    mate = at_q(x, y, 1 - core)

    barrier = pltpu.get_barrier_semaphore()

    def greet(where):
        pl.semaphore_signal(barrier, inc=1, device_id=where, device_id_type=pl.DeviceIdType.MESH)

    for off in range(1, NZ):
        greet(dev(plane(off), q))
    for other in (x_up, x_dn, y_up, y_dn, mate):
        greet(dev(r, other))

    keeps = (q == 0) | (q == 2)
    gives = (q == 1) | (q == 3)

    @pl.when(jnp.logical_not(keeps))
    def _():
        greet(dev(r, p))

    @pl.when(gives)
    def _():
        greet(dev(r, at_q(0, home_y, 0)))

    @pl.when(q < 4)
    def _():
        for t in range(1, 8):
            greet(dev(r, at_q(t % 4, home_y, t // 4)))

    def colb(row):
        return jnp.transpose(jnp.broadcast_to(row, (128, 128)))

    pts = []
    for s in range(4):
        row = piv_ref[s:s + 1, :].astype(F32)
        pts.append(jnp.concatenate([colb(row[:, :128]), colb(row[:, 128:])], axis=0))
    sub = lax.broadcasted_iota(jnp.int32, (NB, 128), 0).astype(F32)
    lane = lax.broadcasted_iota(jnp.int32, (1, 128), 1).astype(F32)

    def swap(cur, s):
        target = sub + float(s * NB)
        delta = pts[s] - target
        move = jnp.where(target == cur, delta, 0.0) - jnp.where(pts[s] == cur, delta, 0.0)
        return cur + jnp.sum(move, axis=0, keepdims=True)

    def perm_tile(t, carry):
        start = lane + (t * 128).astype(F32)
        cur = start
        for s in (3, 2, 1, 0):
            cur = swap(cur, s)
        srcb[pl.ds(pl.multiple_of(t * 128, 128), 128), :] = colb(cur)
        cur = start
        for s in (0, 1, 2, 3):
            cur = swap(cur, s)
        destr[t] = cur
        return carry

    lax.fori_loop(0, 8, perm_tile, 0)

    @pl.when(keeps)
    def _():
        pl.semaphore_wait(barrier, 19)

    @pl.when(gives)
    def _():
        pl.semaphore_wait(barrier, 21)

    @pl.when(q >= 4)
    def _():
        pl.semaphore_wait(barrier, 13)

    groups = ((0, 1), (1, 3), (4, 4))

    def scatter_raw(t, n):
        lo, size = groups[n]
        return rcopy(a_ref.at[pl.ds(lo, size), pl.ds(32 * t, 32), pl.ds(0, NB)],
                     pan.at[pl.ds(lo, size), pl.ds(32 * t, 32), pl.ds(pl.multiple_of(NB * q, NB), NB)],
                     sem_sc.at[8 * n + t], rem_sc.at[n], dev(r, at_q(t % 4, home_y, t // 4)))

    def raw_self(n):
        lo, size = groups[n]
        return pltpu.make_async_copy(
            a_ref.at[pl.ds(lo, size), pl.ds(0, 32), pl.ds(0, NB)],
            pan.at[pl.ds(lo, size), pl.ds(0, 32), pl.ds(pl.multiple_of(NB * q, NB), NB)],
            loc_sem.at[3 + n])

    def raw_start(n):
        @pl.when(keeps)
        def _():
            raw_self(n).start()

        @pl.when(gives)
        def _():
            scatter_raw(0, n).start()

        @pl.when(q < 4)
        def _():
            for t in range(1, 8):
                scatter_raw(t, n).start()

    def raw_wait(n):
        lo, size = groups[n]

        @pl.when(keeps)
        def _():
            raw_self(n).wait()

        @pl.when(jnp.logical_not(keeps))
        def _():
            got(pan.at[pl.ds(lo, size), mine32, minec], sem_sc.at[0], rem_sc.at[n], dev(r, mate))

    def mirror():
        return rcopy(a_ref.at[0, pl.ds(128, 128), :],
                     old_own.at[r % 4, pl.ds(128, 128), :],
                     sem_mir.at[0], rem_mir.at[0], dev(7 - r, q))

    def old_self():
        return pltpu.make_async_copy(a_ref.at[0, pl.ds(0, 128), :],
                                     old_own.at[r % 4, pl.ds(0, 128), :], loc_sem.at[1])

    def contribute(h):
        def body(i, carry):
            cs = pl.ds(4 * i, 4)
            if h == 0:
                for j in range(4):
                    c = 4 * i + j
                    want = srcb[pl.ds(pl.multiple_of(c * 128, 128), 128), :]
                    for t in range(16):
                        gid = lane + ((t // 2 * NZ + r) * NB + (t % 2) * 128).astype(F32)
                        pick[c, :, 128 * t:128 * (t + 1)] = jnp.where(want == gid, 1.0, 0.0).astype(BF)
            rows = dot(pick[cs].reshape(512, 2048), a_ref[:, :, NB * h:NB * (h + 1)].reshape(2048, NB))
            contrib[cs, :, NB * h:NB * (h + 1)] = rows.astype(BF).reshape(4, 128, NB)
            return carry

        lax.fori_loop(0, 2, body, 0)

    def half(h):
        return pl.ds(NB * h, NB)

    def delta(h):
        return 1 if h == 0 else -1

    def rs_send(h, way, k):
        d = delta(h) if way == 0 else -delta(h)
        buf = rs_long if way == 0 else rs_short
        first = 4 if way == 0 else 3
        src = contrib.at[plane(first * d), :, half(h)] if k == 0 else buf.at[h, k - 1]
        idx = h * 7 + way * 4 + k
        return rcopy(src, buf.at[h, k], sem_rs.at[idx], rem_rs.at[idx], dev(plane(d), q))

    def rs_step(h, way, k):
        d = delta(h) if way == 0 else -delta(h)
        buf = rs_long if way == 0 else rs_short
        first = 4 if way == 0 else 3
        rs_send(h, way, k - 1).wait_recv()
        buf[h, k - 1] = buf[h, k - 1] + contrib[plane((first - k) * d), :, NB * h:NB * (h + 1)]
        rs_send(h, way, k).start()

    def rs_end(h):
        rs_send(h, 0, 3).wait_recv()
        rs_send(h, 1, 2).wait_recv()
        top_own[r, :, NB * h:NB * (h + 1)] = (
            contrib[r, :, NB * h:NB * (h + 1)] + rs_long[h, 3] + rs_short[h, 2])

    def top_view(j, h):
        return top_own.at[j, :, half(h)]

    def old_view(j, h):
        hi = j // 4
        a = j + hi * (7 - 2 * j)
        return old_own.at[a, pl.ds(pl.multiple_of(128 * hi, 128), 128), half(h)]

    def zag(view, ssem, rsem, h, way, k):
        d = delta(h) if way == 0 else -delta(h)
        idx = h * 7 + way * 4 + k
        v = view(plane(-k * d), h)
        return rcopy(v, v, ssem.at[idx], rsem.at[idx], dev(plane(d), q))

    def zag_got(view, ssem, rsem, h, way, k):
        d = delta(h) if way == 0 else -delta(h)
        idx = h * 7 + way * 4 + k
        got(view(plane(-(k + 1) * d), h), ssem.at[idx], rsem.at[idx], dev(plane(d), q))

    def zag_step(view, ssem, rsem, h, k):
        for way in range(2):
            if k < 4 - way:
                if k > 0:
                    zag_got(view, ssem, rsem, h, way, k - 1)
                zag(view, ssem, rsem, h, way, k).start()

    def zag_end(view, ssem, rsem, h):
        zag_got(view, ssem, rsem, h, 0, 3)
        zag_got(view, ssem, rsem, h, 1, 2)

    top_z = (top_view, sem_tz, rem_tz)
    old_z = (old_view, sem_dz, rem_dz)

    class Ring:
        def __init__(self, buf, first, n0, rows, base):
            self.buf, self.first, self.n0, self.rows, self.base = buf, first, n0, rows, base

        def reg(self, part, stage, j, piece=None):
            n0, rows = self.n0, self.rows
            lo, n = (0, n0 // 2) if part == 0 else (n0 // 2, n0 // 2)
            if piece is not None:
                n = n // 2
                lo = lo + n * piece
            k = pl.ds(self.first + lo, n)
            along_y = (part == 0) == (stage == 0)
            if stage == 0:
                col = panel_of(j) if along_y else p
                gg = g if along_y else core * 4 + j
                return self.buf.at[k, pl.ds(pl.multiple_of(rows * gg, rows), rows),
                                   pl.ds(pl.multiple_of(NB * col, NB), NB)]
            if part == 0:
                gg = core * 4 + j
                return self.buf.at[k, pl.ds(pl.multiple_of(rows * gg, rows), rows), :]
            return self.buf.at[k, pl.ds(pl.multiple_of(4 * rows * core, 4 * rows), 4 * rows),
                               pl.ds(pl.multiple_of(NB * panel_of(j), NB), NB)]

        def copy(self, part, stage, which):
            along_y = (part == 0) == (stage == 0)
            m = y if along_y else x
            up, dn = (y_up, y_dn) if along_y else (x_up, x_dn)
            idx = self.base + (part * 2 + stage) * 4 + which
            if which < 2:
                v = self.reg(part, stage, m)
            elif which == 2:
                v = self.reg(part, stage, (m + 3) % 4, 0)
            else:
                v = self.reg(part, stage, (m + 1) % 4, 1)
            return rcopy(v, v, sem_ring.at[idx], rem_ring.at[idx], dev(r, up if which % 2 == 0 else dn))

        def wait(self, part, stage, which):
            along_y = (part == 0) == (stage == 0)
            m = y if along_y else x
            idx = self.base + (part * 2 + stage) * 4 + which
            if which == 0:
                v = self.reg(part, stage, (m + 3) % 4)
            elif which == 1:
                v = self.reg(part, stage, (m + 1) % 4)
            else:
                v = self.reg(part, stage, (m + 2) % 4, which - 2)
            got(v, sem_ring.at[idx], rem_ring.at[idx], dev(r, mate))

        def par_view(self, part, piece):
            along_y = part == 1
            m = y if along_y else x
            return m, (0, 3, 1, 2)[piece]

        def par(self, part, piece):
            m, o = self.par_view(part, piece)
            v = self.reg(part, 1, (m + o) % 4)
            idx = self.base // 2 + part * 4 + piece
            return rcopy(v, v, sem_par.at[idx], rem_par.at[idx], dev(r, mate))

        def par_wait(self, part, piece):
            m, o = self.par_view(part, piece)
            v = self.reg_other(part, (m + o) % 4)
            idx = self.base // 2 + part * 4 + piece
            got(v, sem_par.at[idx], rem_par.at[idx], dev(r, mate))

        def reg_other(self, part, j):
            n0, rows = self.n0, self.rows
            oc = 1 - core
            if part == 0:
                gg = oc * 4 + j
                return self.buf.at[pl.ds(self.first, n0 // 2), pl.ds(pl.multiple_of(rows * gg, rows), rows), :]
            return self.buf.at[pl.ds(self.first + n0 // 2, n0 // 2),
                               pl.ds(pl.multiple_of(4 * rows * oc, 4 * rows), 4 * rows),
                               pl.ds(pl.multiple_of(NB * panel_of(j), NB), NB)]

        def start(self, stage, part):
            self.copy(part, stage, 0).start()
            self.copy(part, stage, 1).start()

        def forward(self, stage, part):
            self.wait(part, stage, 0)
            self.copy(part, stage, 2).start()
            self.wait(part, stage, 1)
            self.copy(part, stage, 3).start()
            if stage == 1:
                self.par(part, 1).start()
                self.par(part, 2).start()

        def finish(self, stage, part):
            self.wait(part, stage, 2)
            self.wait(part, stage, 3)
            self.par(part, 0 if stage == 0 else 3).start()

        def close(self, part):
            for piece in range(4):
                self.par_wait(part, piece)

        def drain(self):
            for part in range(2):
                for stage in range(2):
                    for which in range(4):
                        self.copy(part, stage, which).wait_send()
                for piece in range(4):
                    self.par(part, piece).wait_send()

    ring_raw = Ring(pan, 0, 8, 32, 0)
    ring_top = Ring(top_pan, 0, 8, 16, 16)
    ring_old = Ring(pan, 8, 4, 32, 32)

    mine32 = pl.ds(pl.multiple_of(32 * g, 32), 32)
    mine16 = pl.ds(pl.multiple_of(16 * g, 16), 16)
    minec = pl.ds(pl.multiple_of(NB * p, NB), NB)

    def old_slice(off):
        return rcopy(pan.at[0, mine32, minec], pan.at[8 + r % 4, mine32, minec],
                     sem_ds.at[off - 1], rem_ds.at[r % 4], dev(plane(off), q))

    def old_slice_self():
        return pltpu.make_async_copy(pan.at[0, mine32, minec], pan.at[8 + r % 4, mine32, minec],
                                     loc_sem.at[0])

    def top_piece(t):
        return rcopy(top_own.at[r, pl.ds(16 * t, 16), pl.ds(0, NB)],
                     top_pan.at[r, pl.ds(16 * t, 16), pl.ds(pl.multiple_of(NB * q, NB), NB)],
                     sem_ts.at[t], rem_ts.at[0], dev(r, at_q(t % 4, home_y, t // 4)))

    def top_piece_self():
        return pltpu.make_async_copy(
            top_own.at[r, pl.ds(0, 16), pl.ds(0, NB)],
            top_pan.at[r, pl.ds(0, 16), pl.ds(pl.multiple_of(NB * q, NB), NB)], loc_sem.at[2])

    def top_slice(off):
        v = top_pan.at[r, mine16, minec]
        return rcopy(v, v, sem_tsl.at[off - 1], rem_tsl.at[r], dev(plane(off), q))

    row_id = lax.broadcasted_iota(jnp.int32, (NB, 1), 0).astype(F32)

    def find_places(k, carry):
        mine = row_id + ((k * NZ + r) * NB).astype(F32)
        seen = None
        for t in range(8):
            hit = jnp.where(destr[t] == mine, 1.0, 0.0)
            seen = hit if seen is None else seen + hit
            place[k, :, 128 * t:128 * (t + 1)] = hit.astype(BF)
        moved[k] = jnp.broadcast_to(jnp.sum(seen, axis=1, keepdims=True), (NB, 128))
        return carry

    def displaced_own(i, carry):
        ks = pl.ds(2 * i, 2)
        rows = dot(place[ks].reshape(512, TOP), old_own[...].reshape(TOP, COLS)).reshape(2, NB, COLS)
        for j in range(2):
            k = 2 * i + j
            out_ref[k] = jnp.where(moved[k][:, 0:1] > 0.5, rows[j], a_ref[k].astype(F32)).astype(BF)
        return carry

    def displaced_panel(i, carry):
        ks = pl.ds(2 * i, 2)
        rows = dot(place[ks].reshape(512, TOP), pan[8:12].reshape(TOP, TOP))
        left[ks] = rows.astype(BF).reshape(2, NB, TOP)
        return carry

    def top_steps():
        tx[...] = top_pan[...].reshape(TOP, TOP)
        for s in range(3):
            b, e = s * NB, (s + 1) * NB
            l_top = dot(tx[e:, b:e], uinv_ref[s]).astype(BF)
            tx[e:, b:e] = l_top
            u_pan = dot(linv_ref[s], tx[b:e, e:]).astype(BF)
            tx[b:e, e:] = u_pan
            tx[e:, e:] = (tx[e:, e:].astype(F32) - dot(l_top, u_pan)).astype(BF)

    def own_steps():
        ux[...] = top_own[...].reshape(TOP, COLS)
        for s in range(4):
            b, e = s * NB, (s + 1) * NB
            u_own = dot(linv_ref[s], ux[b:e, :]).astype(BF)
            ux[b:e, :] = u_own
            if s < 3:
                ux[e:, :] = (ux[e:, :].astype(F32) - dot(tx[e:, b:e], u_own)).astype(BF)

    TWO = 2

    def below_left(i, carry):
        ks = pl.ds(TWO * i, TWO)
        m = TWO * NB
        for j in range(TWO):
            k = TWO * i + j
            took = moved[k][:, 0:1] > 0.5
            left[k] = jnp.where(took, left[k].astype(F32), pan[k].astype(F32)).astype(BF)
        for s in range(4):
            b, e = s * NB, (s + 1) * NB
            l_row = dot(left[ks, :, b:e].reshape(m, NB), uinv_ref[s]).astype(BF)
            left[ks, :, b:e] = l_row.reshape(TWO, NB, NB)
            if s < 3:
                rest = left[ks, :, e:].reshape(m, TOP - e).astype(F32)
                left[ks, :, e:] = (rest - dot(l_row, tx[b:e, e:])).astype(BF).reshape(TWO, NB, TOP - e)
        return carry

    mycol = pl.ds(pl.multiple_of(NB * jnp.minimum(q, 3), NB), NB)

    def below_rest(i, carry):
        ks = pl.ds(TWO * i, TWO)
        m = TWO * NB
        rest = out_ref[ks].reshape(m, COLS).astype(F32)
        rest = rest - dot(left[ks].reshape(m, TOP), ux[...])
        out_ref[ks] = rest.astype(BF).reshape(TWO, NB, COLS)

        @pl.when(q < 4)
        def _():
            out_ref[ks, :, 0:NB] = left[ks, :, mycol]

        return carry

    def ev_old_send():
        @pl.when(r < 4)
        def _():
            mirror().start()
            old_self().start()

    def ev_old_got():
        @pl.when(r < 4)
        def _():
            old_self().wait()

        @pl.when(r >= 4)
        def _():
            got(old_own.at[(7 - r) % 4, pl.ds(128, 128), :], sem_mir.at[0], rem_mir.at[0], dev(7 - r, q))

    def ev_piece_send():
        @pl.when(keeps)
        def _():
            top_piece_self().start()

        @pl.when(gives)
        def _():
            top_piece(0).start()

        @pl.when(q < 4)
        def _():
            for t in range(1, 8):
                top_piece(t).start()

    def ev_piece_got():
        @pl.when(keeps)
        def _():
            top_piece_self().wait()

        @pl.when(jnp.logical_not(keeps))
        def _():
            got(top_pan.at[r, mine16, minec], sem_ts.at[0], rem_ts.at[0], dev(r, mate))

        for off in range(1, NZ):
            top_slice(off).start()

    def ev_slice_got():
        for off in range(1, NZ):
            src = plane(off)
            got(top_pan.at[src, mine16, minec], sem_tsl.at[0], rem_tsl.at[src], dev(r, mate))

    def ev_oldsl_send():
        @pl.when(r < 4)
        def _():
            old_slice_self().start()
            for off in range(1, NZ):
                old_slice(off).start()

    def ev_oldsl_got():
        for a in range(4):
            @pl.when(r != a)
            def _():
                got(pan.at[8 + a, mine32, minec], sem_ds.at[0], rem_ds.at[a], dev(r, mate))

        @pl.when(r < 4)
        def _():
            old_slice_self().wait()

    def ev_rs0(h):
        rs_send(h, 0, 0).start()
        rs_send(h, 1, 0).start()

    def ev_rs(h, k):
        rs_step(h, 0, k)
        if k < 3:
            rs_step(h, 1, k)

    todo = {
        "C0": lambda: contribute(0), "C1": lambda: contribute(1),
        "os": ev_old_send, "og": ev_old_got, "ps": ev_piece_send, "ph": ev_piece_got,
        "sg": ev_slice_got, "ls": ev_oldsl_send, "lg": ev_oldsl_got,
        "P": lambda: lax.fori_loop(0, 8, find_places, 0),
        "X": lambda: lax.fori_loop(0, 4, displaced_own, 0),
        "Y0": lambda: lax.fori_loop(0, 2, displaced_panel, 0),
        "Y1": lambda: lax.fori_loop(2, 4, displaced_panel, 0),
        "K": top_steps, "U": own_steps,
        "L": lambda: lax.fori_loop(0, 8 // TWO, below_left, 0),
        "F": lambda: lax.fori_loop(0, 8 // TWO, below_rest, 0),
    }
    for n in range(3):
        todo["w%d" % n] = lambda n=n: raw_start(n)
        todo["g%d" % n] = lambda n=n: raw_wait(n)
    for h in range(2):
        todo["r%d0" % h] = lambda h=h: ev_rs0(h)
        for k in range(1, 4):
            todo["r%d%d" % (h, k)] = lambda h=h, k=k: ev_rs(h, k)
        todo["re%d" % h] = lambda h=h: rs_end(h)
        for k in range(4):
            todo["t%d%d" % (h, k)] = lambda h=h, k=k: zag_step(*top_z, h, k)
            todo["d%d%d" % (h, k)] = lambda h=h, k=k: zag_step(*old_z, h, k)
        todo["te%d" % h] = lambda h=h: zag_end(*top_z, h)
        todo["de%d" % h] = lambda h=h: zag_end(*old_z, h)
    for name, ring in (("R", ring_raw), ("S", ring_top), ("O", ring_old)):
        for part in range(2):
            for stage in range(2):
                for verb, f in (("s", ring.start), ("f", ring.forward), ("e", ring.finish)):
                    todo["%s%d%d%s" % (name, part, stage, verb)] = (
                        lambda f=f, stage=stage, part=part: f(stage, part))
            todo["%s%dc" % (name, part)] = lambda ring=ring, part=part: ring.close(part)
    for name in ORDER:
        todo[name]()

    toprow = pl.ds(pl.multiple_of(NB * jnp.minimum(r, 3), NB), NB)

    @pl.when(r < 4)
    def _():
        out_ref[0] = ux[toprow, :]

        @pl.when(q < 4)
        def _():
            out_ref[0, :, 0:NB] = tx[toprow, mycol]

    @pl.when(gives)
    def _():
        for n in range(3):
            scatter_raw(0, n).wait_send()
        top_piece(0).wait_send()

    @pl.when(q < 4)
    def _():
        for t in range(1, 8):
            for n in range(3):
                scatter_raw(t, n).wait_send()
            top_piece(t).wait_send()

    @pl.when(r < 4)
    def _():
        mirror().wait_send()
        for off in range(1, NZ):
            old_slice(off).wait_send()

    for off in range(1, NZ):
        top_slice(off).wait_send()
    for h in range(2):
        for way in range(2):
            for k in range(4 - way):
                rs_send(h, way, k).wait_send()
                zag(*top_z, h, way, k).wait_send()
                zag(*old_z, h, way, k).wait_send()
    ring_raw.drain()
    ring_top.drain()
    ring_old.drain()


def local(matrix, pivots, lower_inverse, upper_inverse):
    rows = matrix.reshape(256, 8, 2, NB).transpose(0, 2, 1, 3)
    a = lax.optimization_barrier(rows).transpose(0, 2, 1, 3).reshape(8, NB, COLS)
    vm = pl.BlockSpec(memory_space=pltpu.VMEM)
    dma = pltpu.SemaphoreType.DMA
    out = pl.pallas_call(
        kernel,
        out_shape=jax.ShapeDtypeStruct((8, NB, COLS), BF),
        in_specs=[vm] * 4,
        out_specs=vm,
        scratch_shapes=[
            pltpu.VMEM((TOP, 128), F32),
            pltpu.VMEM((8, 1, 128), F32),
            pltpu.VMEM((8, 128, COLS), BF),
            pltpu.VMEM((2, 4, 128, NB), BF),
            pltpu.VMEM((2, 3, 128, NB), BF),
            pltpu.VMEM((8, 128, COLS), BF),
            pltpu.VMEM((4, NB, COLS), BF),
            pltpu.VMEM((12, NB, TOP), BF),
            pltpu.VMEM((8, 128, TOP), BF),
            pltpu.VMEM((8, NB, TOP), BF),
            pltpu.VMEM((TOP, TOP), BF),
            pltpu.VMEM((TOP, COLS), BF),
            pltpu.VMEM((8, 128, 2048), BF),
            pltpu.VMEM((8, NB, TOP), BF),
            pltpu.VMEM((8, NB, 128), F32),
            dma((14,)), dma((14,)), dma((14,)), dma((14,)), dma((14,)), dma((14,)),
            dma((24,)), dma((3,)), dma((1,)), dma((1,)), dma((6,)), dma((7,)), dma((4,)),
            dma((8,)), dma((1,)), dma((7,)), dma((8,)),
            dma((48,)), dma((48,)), dma((24,)), dma((24,)),
        ],
        compiler_params=pltpu.CompilerParams(
            collective_id=0, has_side_effects=True, vmem_limit_bytes=46 * 1024 * 1024),
    )(a, pivots, lower_inverse, upper_inverse)
    return out.reshape(matrix.shape)


def solution(mesh):
    placed = (P(None, "prow", None, "pcol"), P(), P(), P())
    return jax.shard_map(
        local, mesh=mesh, in_specs=placed, out_specs=P(None, "prow", None, "pcol"), check_vma=False
    )
```

```python
import jax
import jax.numpy as jnp
from jax import lax
from jax.experimental import pallas as pl
from jax.experimental.pallas import tpu as pltpu
from jax.sharding import PartitionSpec as P

BF = jnp.bfloat16
F32 = jnp.float32
NB = 256
NZ = 8
TOP = 1024
COLS = 512


ORDER = ('w0', 'w1', 'w2', 'os', 'C0', 'r00', 'C1', 'r10', 'g0', 'ls', 'r01', 'g1', 'R00s', 'P', 'r11', 'lg', 'O00s', 'O10s', 'R00f', 'r02', 'r12', 'g2', 'R10s', 'R00e', 'O00f', 'O10f', 'r03', 'r13', 'og', 'd00', 'd10', 'R10f', 're0', 'ps', 're1', 'O00e', 'O10e', 'O01s', 'O11s', 'R10e', 'R01s', 'R11s', 'ph', 'd01', 'd11', 't00', 't10', 'O01f', 'O11f', 'sg', 'S00s', 'S10s', 'd02', 'd12', 't01', 't11', 'O01e', 'O11e', 'O0c', 'O1c', 'S00f', 'S10f', 'd03', 'd13', 'Y0', 'R01f', 'R11f', 't02', 't12', 'S00e', 'S10e', 'S01s', 'S11s', 'Y1', 'de0', 'de1', 't03', 't13', 'S01f', 'S11f', 'X', 'R01e', 'R11e', 'S01e', 'S11e', 'R0c', 'R1c', 'S0c', 'S1c', 'K', 'L', 'te0', 'te1', 'U', 'F')


def dot(a, b):
    return jnp.dot(a, b, preferred_element_type=F32)


def kernel(a_ref, piv_ref, linv_ref, uinv_ref, out_ref,
           srcb, destr, contrib, rs_long, rs_short, top_own, old_own, pan, top_pan,
           left, tx, ux, pick, place, moved,
           sem_rs, rem_rs, sem_tz, rem_tz, sem_dz, rem_dz,
           sem_sc, rem_sc, sem_mir, rem_mir, loc_sem, sem_ds, rem_ds,
           sem_ts, rem_ts, sem_tsl, rem_tsl,
           sem_ring, rem_ring, sem_par, rem_par):
    r = lax.axis_index("prow")
    q = lax.axis_index("pcol")
    x = q // 8
    y = (q // 2) % 4
    core = q % 2
    g = core * 4 + x

    def panel_of(yy):
        return (yy % 3 + 1) * ((yy + 3) // 4)

    p = panel_of(y)
    home_y = ((q + 1) % 3 + 1) * ((q + 3) // 4)

    def dev(rr, qq):
        return (rr, qq)

    def at_q(xx, yy, cc):
        return xx * 8 + yy * 2 + cc

    def plane(off):
        return (r + off + NZ) % NZ

    def rcopy(src, dst, ssem, rsem, where):
        return pltpu.make_async_remote_copy(
            src_ref=src, dst_ref=dst, send_sem=ssem, recv_sem=rsem,
            device_id=where, device_id_type=pl.DeviceIdType.MESH)

    def got(dst, ssem, rsem, where):
        rcopy(dst, dst, ssem, rsem, where).wait_recv()

    def sent(src, ssem, rsem, where):
        rcopy(src, src, ssem, rsem, where).wait_send()

    x_up, x_dn = at_q((x + 1) % 4, y, core), at_q((x + 3) % 4, y, core)
    y_up, y_dn = at_q(x, (y + 1) % 4, core), at_q(x, (y + 3) % 4, core)
    mate = at_q(x, y, 1 - core)

    barrier = pltpu.get_barrier_semaphore()

    def greet(where):
        pl.semaphore_signal(barrier, inc=1, device_id=where, device_id_type=pl.DeviceIdType.MESH)

    for off in range(1, NZ):
        greet(dev(plane(off), q))
    for other in (x_up, x_dn, y_up, y_dn, mate):
        greet(dev(r, other))

    keeps = (q == 0) | (q == 2)
    gives = (q == 1) | (q == 3)

    @pl.when(jnp.logical_not(keeps))
    def _():
        greet(dev(r, p))

    @pl.when(gives)
    def _():
        greet(dev(r, at_q(0, home_y, 0)))

    @pl.when(q < 4)
    def _():
        for t in range(1, 8):
            greet(dev(r, at_q(t % 4, home_y, t // 4)))

    def colb(row):
        return jnp.transpose(jnp.broadcast_to(row, (128, 128)))

    pts = []
    for s in range(4):
        row = piv_ref[s:s + 1, :].astype(F32)
        pts.append(jnp.concatenate([colb(row[:, :128]), colb(row[:, 128:])], axis=0))
    sub = lax.broadcasted_iota(jnp.int32, (NB, 128), 0).astype(F32)
    lane = lax.broadcasted_iota(jnp.int32, (1, 128), 1).astype(F32)

    def swap(cur, s):
        target = sub + float(s * NB)
        delta = pts[s] - target
        move = jnp.where(target == cur, delta, 0.0) - jnp.where(pts[s] == cur, delta, 0.0)
        return cur + jnp.sum(move, axis=0, keepdims=True)

    def perm_tile(t, carry):
        start = lane + (t * 128).astype(F32)
        cur = start
        for s in (3, 2, 1, 0):
            cur = swap(cur, s)
        srcb[pl.ds(pl.multiple_of(t * 128, 128), 128), :] = colb(cur)
        cur = start
        for s in (0, 1, 2, 3):
            cur = swap(cur, s)
        destr[t] = cur
        return carry

    lax.fori_loop(0, 8, perm_tile, 0)

    @pl.when(keeps)
    def _():
        pl.semaphore_wait(barrier, 19)

    @pl.when(gives)
    def _():
        pl.semaphore_wait(barrier, 21)

    @pl.when(q >= 4)
    def _():
        pl.semaphore_wait(barrier, 13)

    groups = ((0, 1), (1, 3), (4, 4))

    def scatter_raw(t, n):
        lo, size = groups[n]
        return rcopy(a_ref.at[pl.ds(lo, size), pl.ds(32 * t, 32), pl.ds(0, NB)],
                     pan.at[pl.ds(lo, size), pl.ds(32 * t, 32), pl.ds(pl.multiple_of(NB * q, NB), NB)],
                     sem_sc.at[8 * n + t], rem_sc.at[n], dev(r, at_q(t % 4, home_y, t // 4)))

    def raw_self(n):
        lo, size = groups[n]
        return pltpu.make_async_copy(
            a_ref.at[pl.ds(lo, size), pl.ds(0, 32), pl.ds(0, NB)],
            pan.at[pl.ds(lo, size), pl.ds(0, 32), pl.ds(pl.multiple_of(NB * q, NB), NB)],
            loc_sem.at[3 + n])

    def raw_start(n):
        @pl.when(keeps)
        def _():
            raw_self(n).start()

        @pl.when(gives)
        def _():
            scatter_raw(0, n).start()

        @pl.when(q < 4)
        def _():
            for t in range(1, 8):
                scatter_raw(t, n).start()

    def raw_wait(n):
        lo, size = groups[n]

        @pl.when(keeps)
        def _():
            raw_self(n).wait()

        @pl.when(jnp.logical_not(keeps))
        def _():
            got(pan.at[pl.ds(lo, size), mine32, minec], sem_sc.at[0], rem_sc.at[n], dev(r, mate))

    def mirror():
        return rcopy(a_ref.at[0, pl.ds(128, 128), :],
                     old_own.at[r % 4, pl.ds(128, 128), :],
                     sem_mir.at[0], rem_mir.at[0], dev(7 - r, q))

    def old_self():
        return pltpu.make_async_copy(a_ref.at[0, pl.ds(0, 128), :],
                                     old_own.at[r % 4, pl.ds(0, 128), :], loc_sem.at[1])

    def contribute(h):
        def body(i, carry):
            cs = pl.ds(4 * i, 4)
            if h == 0:
                for j in range(4):
                    c = 4 * i + j
                    want = srcb[pl.ds(pl.multiple_of(c * 128, 128), 128), :]
                    for t in range(16):
                        gid = lane + ((t // 2 * NZ + r) * NB + (t % 2) * 128).astype(F32)
                        pick[c, :, 128 * t:128 * (t + 1)] = jnp.where(want == gid, 1.0, 0.0).astype(BF)
            rows = dot(pick[cs].reshape(512, 2048), a_ref[:, :, NB * h:NB * (h + 1)].reshape(2048, NB))
            contrib[cs, :, NB * h:NB * (h + 1)] = rows.astype(BF).reshape(4, 128, NB)
            return carry

        lax.fori_loop(0, 2, body, 0)

    def half(h):
        return pl.ds(NB * h, NB)

    def delta(h):
        return 1 if h == 0 else -1

    def rs_send(h, way, k):
        d = delta(h) if way == 0 else -delta(h)
        buf = rs_long if way == 0 else rs_short
        first = 4 if way == 0 else 3
        src = contrib.at[plane(first * d), :, half(h)] if k == 0 else buf.at[h, k - 1]
        idx = h * 7 + way * 4 + k
        return rcopy(src, buf.at[h, k], sem_rs.at[idx], rem_rs.at[idx], dev(plane(d), q))

    def rs_step(h, way, k):
        d = delta(h) if way == 0 else -delta(h)
        buf = rs_long if way == 0 else rs_short
        first = 4 if way == 0 else 3
        rs_send(h, way, k - 1).wait_recv()
        buf[h, k - 1] = buf[h, k - 1] + contrib[plane((first - k) * d), :, NB * h:NB * (h + 1)]
        rs_send(h, way, k).start()

    def rs_end(h):
        rs_send(h, 0, 3).wait_recv()
        rs_send(h, 1, 2).wait_recv()
        top_own[r, :, NB * h:NB * (h + 1)] = (
            contrib[r, :, NB * h:NB * (h + 1)] + rs_long[h, 3] + rs_short[h, 2])

    def top_view(j, h):
        return top_own.at[j, :, half(h)]

    def old_view(j, h):
        hi = j // 4
        a = j + hi * (7 - 2 * j)
        return old_own.at[a, pl.ds(pl.multiple_of(128 * hi, 128), 128), half(h)]

    def zag(view, ssem, rsem, h, way, k):
        d = delta(h) if way == 0 else -delta(h)
        idx = h * 7 + way * 4 + k
        v = view(plane(-k * d), h)
        return rcopy(v, v, ssem.at[idx], rsem.at[idx], dev(plane(d), q))

    def zag_got(view, ssem, rsem, h, way, k):
        d = delta(h) if way == 0 else -delta(h)
        idx = h * 7 + way * 4 + k
        got(view(plane(-(k + 1) * d), h), ssem.at[idx], rsem.at[idx], dev(plane(d), q))

    def zag_step(view, ssem, rsem, h, k):
        for way in range(2):
            if k < 4 - way:
                if k > 0:
                    zag_got(view, ssem, rsem, h, way, k - 1)
                zag(view, ssem, rsem, h, way, k).start()

    def zag_end(view, ssem, rsem, h):
        zag_got(view, ssem, rsem, h, 0, 3)
        zag_got(view, ssem, rsem, h, 1, 2)

    top_z = (top_view, sem_tz, rem_tz)
    old_z = (old_view, sem_dz, rem_dz)

    class Ring:
        def __init__(self, buf, first, n0, rows, base):
            self.buf, self.first, self.n0, self.rows, self.base = buf, first, n0, rows, base

        def reg(self, part, stage, j, piece=None):
            n0, rows = self.n0, self.rows
            lo, n = (0, n0 // 2) if part == 0 else (n0 // 2, n0 // 2)
            if piece is not None:
                n = n // 2
                lo = lo + n * piece
            k = pl.ds(self.first + lo, n)
            along_y = (part == 0) == (stage == 0)
            if stage == 0:
                col = panel_of(j) if along_y else p
                gg = g if along_y else core * 4 + j
                return self.buf.at[k, pl.ds(pl.multiple_of(rows * gg, rows), rows),
                                   pl.ds(pl.multiple_of(NB * col, NB), NB)]
            if part == 0:
                gg = core * 4 + j
                return self.buf.at[k, pl.ds(pl.multiple_of(rows * gg, rows), rows), :]
            return self.buf.at[k, pl.ds(pl.multiple_of(4 * rows * core, 4 * rows), 4 * rows),
                               pl.ds(pl.multiple_of(NB * panel_of(j), NB), NB)]

        def copy(self, part, stage, which):
            along_y = (part == 0) == (stage == 0)
            m = y if along_y else x
            up, dn = (y_up, y_dn) if along_y else (x_up, x_dn)
            idx = self.base + (part * 2 + stage) * 4 + which
            if which < 2:
                v = self.reg(part, stage, m)
            elif which == 2:
                v = self.reg(part, stage, (m + 3) % 4, 0)
            else:
                v = self.reg(part, stage, (m + 1) % 4, 1)
            return rcopy(v, v, sem_ring.at[idx], rem_ring.at[idx], dev(r, up if which % 2 == 0 else dn))

        def wait(self, part, stage, which):
            along_y = (part == 0) == (stage == 0)
            m = y if along_y else x
            idx = self.base + (part * 2 + stage) * 4 + which
            if which == 0:
                v = self.reg(part, stage, (m + 3) % 4)
            elif which == 1:
                v = self.reg(part, stage, (m + 1) % 4)
            else:
                v = self.reg(part, stage, (m + 2) % 4, which - 2)
            got(v, sem_ring.at[idx], rem_ring.at[idx], dev(r, mate))

        def par_view(self, part, piece):
            along_y = part == 1
            m = y if along_y else x
            return m, (0, 3, 1, 2)[piece]

        def par(self, part, piece):
            m, o = self.par_view(part, piece)
            v = self.reg(part, 1, (m + o) % 4)
            idx = self.base // 2 + part * 4 + piece
            return rcopy(v, v, sem_par.at[idx], rem_par.at[idx], dev(r, mate))

        def par_wait(self, part, piece):
            m, o = self.par_view(part, piece)
            v = self.reg_other(part, (m + o) % 4)
            idx = self.base // 2 + part * 4 + piece
            got(v, sem_par.at[idx], rem_par.at[idx], dev(r, mate))

        def reg_other(self, part, j):
            n0, rows = self.n0, self.rows
            oc = 1 - core
            if part == 0:
                gg = oc * 4 + j
                return self.buf.at[pl.ds(self.first, n0 // 2), pl.ds(pl.multiple_of(rows * gg, rows), rows), :]
            return self.buf.at[pl.ds(self.first + n0 // 2, n0 // 2),
                               pl.ds(pl.multiple_of(4 * rows * oc, 4 * rows), 4 * rows),
                               pl.ds(pl.multiple_of(NB * panel_of(j), NB), NB)]

        def start(self, stage, part):
            self.copy(part, stage, 0).start()
            self.copy(part, stage, 1).start()

        def forward(self, stage, part):
            self.wait(part, stage, 0)
            self.copy(part, stage, 2).start()
            self.wait(part, stage, 1)
            self.copy(part, stage, 3).start()
            if stage == 1:
                self.par(part, 1).start()
                self.par(part, 2).start()

        def finish(self, stage, part):
            self.wait(part, stage, 2)
            self.wait(part, stage, 3)
            self.par(part, 0 if stage == 0 else 3).start()

        def close(self, part):
            for piece in range(4):
                self.par_wait(part, piece)

        def drain(self):
            for part in range(2):
                for stage in range(2):
                    for which in range(4):
                        self.copy(part, stage, which).wait_send()
                for piece in range(4):
                    self.par(part, piece).wait_send()

    ring_raw = Ring(pan, 0, 8, 32, 0)
    ring_top = Ring(top_pan, 0, 8, 16, 16)
    ring_old = Ring(pan, 8, 4, 32, 32)

    mine32 = pl.ds(pl.multiple_of(32 * g, 32), 32)
    mine16 = pl.ds(pl.multiple_of(16 * g, 16), 16)
    minec = pl.ds(pl.multiple_of(NB * p, NB), NB)

    def old_slice(off):
        return rcopy(pan.at[0, mine32, minec], pan.at[8 + r % 4, mine32, minec],
                     sem_ds.at[off - 1], rem_ds.at[r % 4], dev(plane(off), q))

    def old_slice_self():
        return pltpu.make_async_copy(pan.at[0, mine32, minec], pan.at[8 + r % 4, mine32, minec],
                                     loc_sem.at[0])

    def top_piece(t):
        return rcopy(top_own.at[r, pl.ds(16 * t, 16), pl.ds(0, NB)],
                     top_pan.at[r, pl.ds(16 * t, 16), pl.ds(pl.multiple_of(NB * q, NB), NB)],
                     sem_ts.at[t], rem_ts.at[0], dev(r, at_q(t % 4, home_y, t // 4)))

    def top_piece_self():
        return pltpu.make_async_copy(
            top_own.at[r, pl.ds(0, 16), pl.ds(0, NB)],
            top_pan.at[r, pl.ds(0, 16), pl.ds(pl.multiple_of(NB * q, NB), NB)], loc_sem.at[2])

    def top_slice(off):
        v = top_pan.at[r, mine16, minec]
        return rcopy(v, v, sem_tsl.at[off - 1], rem_tsl.at[r], dev(plane(off), q))

    row_id = lax.broadcasted_iota(jnp.int32, (NB, 1), 0).astype(F32)

    def find_places(k, carry):
        mine = row_id + ((k * NZ + r) * NB).astype(F32)
        seen = None
        for t in range(8):
            hit = jnp.where(destr[t] == mine, 1.0, 0.0)
            seen = hit if seen is None else seen + hit
            place[k, :, 128 * t:128 * (t + 1)] = hit.astype(BF)
        moved[k] = jnp.broadcast_to(jnp.sum(seen, axis=1, keepdims=True), (NB, 128))
        return carry

    def displaced_own(i, carry):
        ks = pl.ds(2 * i, 2)
        rows = dot(place[ks].reshape(512, TOP), old_own[...].reshape(TOP, COLS)).reshape(2, NB, COLS)
        for j in range(2):
            k = 2 * i + j
            out_ref[k] = jnp.where(moved[k][:, 0:1] > 0.5, rows[j], a_ref[k].astype(F32)).astype(BF)
        return carry

    def displaced_panel(i, carry):
        ks = pl.ds(2 * i, 2)
        rows = dot(place[ks].reshape(512, TOP), pan[8:12].reshape(TOP, TOP))
        left[ks] = rows.astype(BF).reshape(2, NB, TOP)
        return carry

    def top_steps():
        tx[...] = top_pan[...].reshape(TOP, TOP)
        for s in range(3):
            b, e = s * NB, (s + 1) * NB
            l_top = dot(tx[e:, b:e], uinv_ref[s]).astype(BF)
            tx[e:, b:e] = l_top
            u_pan = dot(linv_ref[s], tx[b:e, e:]).astype(BF)
            tx[b:e, e:] = u_pan
            tx[e:, e:] = (tx[e:, e:].astype(F32) - dot(l_top, u_pan)).astype(BF)

    def own_steps():
        ux[...] = top_own[...].reshape(TOP, COLS)
        for s in range(4):
            b, e = s * NB, (s + 1) * NB
            u_own = dot(linv_ref[s], ux[b:e, :]).astype(BF)
            ux[b:e, :] = u_own
            if s < 3:
                ux[e:, :] = (ux[e:, :].astype(F32) - dot(tx[e:, b:e], u_own)).astype(BF)

    TWO = 4

    def below_left(i, carry):
        ks = pl.ds(TWO * i, TWO)
        m = TWO * NB
        for j in range(TWO):
            k = TWO * i + j
            took = moved[k][:, 0:1] > 0.5
            left[k] = jnp.where(took, left[k].astype(F32), pan[k].astype(F32)).astype(BF)
        for s in range(4):
            b, e = s * NB, (s + 1) * NB
            l_row = dot(left[ks, :, b:e].reshape(m, NB), uinv_ref[s]).astype(BF)
            left[ks, :, b:e] = l_row.reshape(TWO, NB, NB)
            if s < 3:
                rest = left[ks, :, e:].reshape(m, TOP - e).astype(F32)
                left[ks, :, e:] = (rest - dot(l_row, tx[b:e, e:])).astype(BF).reshape(TWO, NB, TOP - e)
        return carry

    mycol = pl.ds(pl.multiple_of(NB * jnp.minimum(q, 3), NB), NB)

    def below_rest(i, carry):
        ks = pl.ds(TWO * i, TWO)
        m = TWO * NB
        rest = out_ref[ks].reshape(m, COLS).astype(F32)
        rest = rest - dot(left[ks].reshape(m, TOP), ux[...])
        out_ref[ks] = rest.astype(BF).reshape(TWO, NB, COLS)

        @pl.when(q < 4)
        def _():
            out_ref[ks, :, 0:NB] = left[ks, :, mycol]

        return carry

    def ev_old_send():
        @pl.when(r < 4)
        def _():
            mirror().start()
            old_self().start()

    def ev_old_got():
        @pl.when(r < 4)
        def _():
            old_self().wait()

        @pl.when(r >= 4)
        def _():
            got(old_own.at[(7 - r) % 4, pl.ds(128, 128), :], sem_mir.at[0], rem_mir.at[0], dev(7 - r, q))

    def ev_piece_send():
        @pl.when(keeps)
        def _():
            top_piece_self().start()

        @pl.when(gives)
        def _():
            top_piece(0).start()

        @pl.when(q < 4)
        def _():
            for t in range(1, 8):
                top_piece(t).start()

    def ev_piece_got():
        @pl.when(keeps)
        def _():
            top_piece_self().wait()

        @pl.when(jnp.logical_not(keeps))
        def _():
            got(top_pan.at[r, mine16, minec], sem_ts.at[0], rem_ts.at[0], dev(r, mate))

        for off in range(1, NZ):
            top_slice(off).start()

    def ev_slice_got():
        for off in range(1, NZ):
            src = plane(off)
            got(top_pan.at[src, mine16, minec], sem_tsl.at[0], rem_tsl.at[src], dev(r, mate))

    def ev_oldsl_send():
        @pl.when(r < 4)
        def _():
            old_slice_self().start()
            for off in range(1, NZ):
                old_slice(off).start()

    def ev_oldsl_got():
        for a in range(4):
            @pl.when(r != a)
            def _():
                got(pan.at[8 + a, mine32, minec], sem_ds.at[0], rem_ds.at[a], dev(r, mate))

        @pl.when(r < 4)
        def _():
            old_slice_self().wait()

    def ev_rs0(h):
        rs_send(h, 0, 0).start()
        rs_send(h, 1, 0).start()

    def ev_rs(h, k):
        rs_step(h, 0, k)
        if k < 3:
            rs_step(h, 1, k)

    todo = {
        "C0": lambda: contribute(0), "C1": lambda: contribute(1),
        "os": ev_old_send, "og": ev_old_got, "ps": ev_piece_send, "ph": ev_piece_got,
        "sg": ev_slice_got, "ls": ev_oldsl_send, "lg": ev_oldsl_got,
        "P": lambda: lax.fori_loop(0, 8, find_places, 0),
        "X": lambda: lax.fori_loop(0, 4, displaced_own, 0),
        "Y0": lambda: lax.fori_loop(0, 2, displaced_panel, 0),
        "Y1": lambda: lax.fori_loop(2, 4, displaced_panel, 0),
        "K": top_steps, "U": own_steps,
        "L": lambda: lax.fori_loop(0, 8 // TWO, below_left, 0),
        "F": lambda: lax.fori_loop(0, 8 // TWO, below_rest, 0),
    }
    for n in range(3):
        todo["w%d" % n] = lambda n=n: raw_start(n)
        todo["g%d" % n] = lambda n=n: raw_wait(n)
    for h in range(2):
        todo["r%d0" % h] = lambda h=h: ev_rs0(h)
        for k in range(1, 4):
            todo["r%d%d" % (h, k)] = lambda h=h, k=k: ev_rs(h, k)
        todo["re%d" % h] = lambda h=h: rs_end(h)
        for k in range(4):
            todo["t%d%d" % (h, k)] = lambda h=h, k=k: zag_step(*top_z, h, k)
            todo["d%d%d" % (h, k)] = lambda h=h, k=k: zag_step(*old_z, h, k)
        todo["te%d" % h] = lambda h=h: zag_end(*top_z, h)
        todo["de%d" % h] = lambda h=h: zag_end(*old_z, h)
    for name, ring in (("R", ring_raw), ("S", ring_top), ("O", ring_old)):
        for part in range(2):
            for stage in range(2):
                for verb, f in (("s", ring.start), ("f", ring.forward), ("e", ring.finish)):
                    todo["%s%d%d%s" % (name, part, stage, verb)] = (
                        lambda f=f, stage=stage, part=part: f(stage, part))
            todo["%s%dc" % (name, part)] = lambda ring=ring, part=part: ring.close(part)
    for name in ORDER:
        todo[name]()

    toprow = pl.ds(pl.multiple_of(NB * jnp.minimum(r, 3), NB), NB)

    @pl.when(r < 4)
    def _():
        out_ref[0] = ux[toprow, :]

        @pl.when(q < 4)
        def _():
            out_ref[0, :, 0:NB] = tx[toprow, mycol]

    @pl.when(gives)
    def _():
        for n in range(3):
            scatter_raw(0, n).wait_send()
        top_piece(0).wait_send()

    @pl.when(q < 4)
    def _():
        for t in range(1, 8):
            for n in range(3):
                scatter_raw(t, n).wait_send()
            top_piece(t).wait_send()

    @pl.when(r < 4)
    def _():
        mirror().wait_send()
        for off in range(1, NZ):
            old_slice(off).wait_send()

    for off in range(1, NZ):
        top_slice(off).wait_send()
    for h in range(2):
        for way in range(2):
            for k in range(4 - way):
                rs_send(h, way, k).wait_send()
                zag(*top_z, h, way, k).wait_send()
                zag(*old_z, h, way, k).wait_send()
    ring_raw.drain()
    ring_top.drain()
    ring_old.drain()


def local(matrix, pivots, lower_inverse, upper_inverse):
    rows = matrix.reshape(256, 8, 2, NB).transpose(0, 2, 1, 3)
    a = lax.optimization_barrier(rows).transpose(0, 2, 1, 3).reshape(8, NB, COLS)
    vm = pl.BlockSpec(memory_space=pltpu.VMEM)
    dma = pltpu.SemaphoreType.DMA
    out = pl.pallas_call(
        kernel,
        out_shape=jax.ShapeDtypeStruct((8, NB, COLS), BF),
        in_specs=[vm] * 4,
        out_specs=vm,
        scratch_shapes=[
            pltpu.VMEM((TOP, 128), F32),
            pltpu.VMEM((8, 1, 128), F32),
            pltpu.VMEM((8, 128, COLS), BF),
            pltpu.VMEM((2, 4, 128, NB), BF),
            pltpu.VMEM((2, 3, 128, NB), BF),
            pltpu.VMEM((8, 128, COLS), BF),
            pltpu.VMEM((4, NB, COLS), BF),
            pltpu.VMEM((12, NB, TOP), BF),
            pltpu.VMEM((8, 128, TOP), BF),
            pltpu.VMEM((8, NB, TOP), BF),
            pltpu.VMEM((TOP, TOP), BF),
            pltpu.VMEM((TOP, COLS), BF),
            pltpu.VMEM((8, 128, 2048), BF),
            pltpu.VMEM((8, NB, TOP), BF),
            pltpu.VMEM((8, NB, 128), F32),
            dma((14,)), dma((14,)), dma((14,)), dma((14,)), dma((14,)), dma((14,)),
            dma((24,)), dma((3,)), dma((1,)), dma((1,)), dma((6,)), dma((7,)), dma((4,)),
            dma((8,)), dma((1,)), dma((7,)), dma((8,)),
            dma((48,)), dma((48,)), dma((24,)), dma((24,)),
        ],
        compiler_params=pltpu.CompilerParams(
            collective_id=0, has_side_effects=True, vmem_limit_bytes=46 * 1024 * 1024),
    )(a, pivots, lower_inverse, upper_inverse)
    return out.reshape(matrix.shape)


def solution(mesh):
    placed = (P(None, "prow", None, "pcol"), P(), P(), P())
    return jax.shard_map(
        local, mesh=mesh, in_specs=placed, out_specs=P(None, "prow", None, "pcol"), check_vma=False
    )
```
